32 devices in a mesh: ang: 4 (over y, x), snap: 8 (over z, core).
Axes of the slice: x: 2, y: 2, z: 4, core: 2. Of those that a mesh axis runs over, the one named last changes fastest.
Arguments:
- cube: bfloat16 [2, 512, 8192], P(None, None, 'snap'), may hold values from -24 to 24
- select: int32 [1024], P('snap'), may hold values from 0 to 8191, as said below
- phases: int32 [16], replicated, may hold values from 0 to 63
- jitter: float32 [2, 512], replicated, may hold values from -0.4 to 0.4
Outputs:
- powers: float32 [16384], P(('ang', 'snap'))
The draws below stay inside these ranges and needn't reach their ends.
Inputs may be any that keep to these rules, and one draw needn't show every extreme that they name: `select`: the selections of snapshot block j (entries j * 128 to (j + 1) * 128 - 1) lie in cell block j (cells j * 1024 to (j + 1) * 1024 - 1).
All inputs are finite; a program needn't handle non-finite values.
Results may differ from the reference program's by a relative error of at most 0.0012.
Values sent between devices are 32-bit elements; how exact they have to be, the bound alone decides.
No kernel may reach another device: no remote copies, remote signals or barrier semaphores. Data moves between devices by JAX's collectives and lax.ppermute only.
A program may use at most 128 MiB of HBM per device.

```python
import math
import jax
import jax.numpy as jnp
from jax import lax

TX = 16
RX = 32
GU = 128
GV = 128
Q = 64
ITERS = 3
S_DEV = 128
M = 512
K = 16384
POOL_DEV = 1024
SNAPS = 1024
N_ANG = 4
N_SNAP = 8


emitters = 48


def scene(key):
    phase_steps = jax.random.randint(jax.random.fold_in(key, 11), (TX,), 0, Q)
    row_index = jax.random.randint(jax.random.fold_in(key, 12), (emitters,), 0, GU)
    col_index = jax.random.randint(jax.random.fold_in(key, 13), (emitters,), 0, GV)
    offsets = jax.random.uniform(jax.random.fold_in(key, 14), (2, TX * RX), jnp.float32, -0.4, 0.4)
    return (phase_steps, row_index, col_index, offsets)


def draw_phases(key, part):
    return scene(key)[0].astype(jnp.int32)


def draw_jitter(key, part):
    return scene(key)[3].astype(jnp.float32)


def draw_select(key, part):
    offsets = jax.random.randint(jax.random.fold_in(key, 21), (SNAPS,), 0, POOL_DEV)
    blocks = jnp.arange(SNAPS, dtype=jnp.int32) // S_DEV
    return (blocks * POOL_DEV + offsets).astype(jnp.int32)


def draw_cube(key, part):
    phase_steps, row_index, col_index, shifts = scene(key)
    channels = TX * RX
    channel = jnp.arange(channels, dtype=jnp.int32)
    position_x = (channel % RX).astype(jnp.float32) + shifts[0]
    position_y = (channel // RX).astype(jnp.float32) + shifts[1]
    row_angle = (2 * row_index - GU).astype(jnp.float32) / GU
    col_angle = (2 * col_index - GV).astype(jnp.float32) / GV
    offsets = jnp.take(phase_steps, channel // RX).astype(jnp.float32)
    phase_angle = math.pi * (position_x[:, None] * row_angle[None, :] + position_y[:, None] * col_angle[None, :])
    phase_angle = phase_angle + 2.0 * math.pi / Q * offsets[:, None]
    amplitude = jnp.exp(jax.random.uniform(jax.random.fold_in(key, 31), (emitters,), jnp.float32, math.log(0.1), 0.0))
    rising = 3.0
    cells = POOL_DEV * N_SNAP
    ramp = jnp.sqrt(1.0 + (rising - 1.0) * jnp.arange(cells, dtype=jnp.float32) / max(cells - 1, 1))
    signal_re = jax.random.normal(jax.random.fold_in(key, 32), (emitters, cells), jnp.float32) * amplitude[:, None] * ramp[None, :]
    signal_im = jax.random.normal(jax.random.fold_in(key, 33), (emitters, cells), jnp.float32) * amplitude[:, None] * ramp[None, :]
    cosine = jnp.cos(phase_angle)
    sine = jnp.sin(phase_angle)
    data_re = jnp.dot(cosine, signal_re, precision=jax.lax.Precision.HIGHEST) - jnp.dot(sine, signal_im, precision=jax.lax.Precision.HIGHEST)
    data_im = jnp.dot(cosine, signal_im, precision=jax.lax.Precision.HIGHEST) + jnp.dot(sine, signal_re, precision=jax.lax.Precision.HIGHEST)
    noise = jax.random.normal(jax.random.fold_in(key, 34), (2, channels, cells), jnp.float32) * ramp[None, None, :]
    result = jnp.stack([data_re, data_im]) + noise
    return jnp.clip(result, -24.0, 24.0).astype(jnp.bfloat16)


def setup_inputs(seed: int = 0) -> dict:
    splits = jax.random.split(jax.random.key(seed), 5)
    cube = draw_cube(jax.random.fold_in(splits[4], 71), 0)
    select = draw_select(jax.random.fold_in(splits[4], 71), 0)
    phases = draw_phases(jax.random.fold_in(splits[4], 71), 0)
    jitter = draw_jitter(jax.random.fold_in(splits[4], 71), 0)
    return {"cube": cube, "select": select, "phases": phases, "jitter": jitter}


def steering_block(columns, phases, jitter, receivers):
    channels = phases.shape[0] * receivers
    channel = jnp.arange(channels, dtype=jnp.int32)
    position_x = (channel % receivers).astype(jnp.float32) + jitter[0]
    position_y = (channel // receivers).astype(jnp.float32) + jitter[1]
    offsets = jnp.broadcast_to(phases[:, None], (phases.shape[0], receivers)).reshape(channels)
    row_angle = (2 * (columns // GV) - GU).astype(jnp.float32) / GU
    col_angle = (2 * (columns % GV) - GV).astype(jnp.float32) / GV
    phase_angle = math.pi * (position_x[:, None] * row_angle[None, :] + position_y[:, None] * col_angle[None, :])
    phase_angle = phase_angle + 2.0 * math.pi / Q * offsets.astype(jnp.float32)[:, None]
    return jnp.stack([jnp.cos(phase_angle), jnp.sin(phase_angle)]).astype(jnp.bfloat16)

def beam_power(steering, samples):
    rows = steering.shape[0] * steering.shape[1]
    flat = steering.reshape(rows, steering.shape[2])
    turned = jnp.concatenate([samples[1], -samples[0]], axis=0)
    paired = jnp.concatenate([samples.reshape(rows, samples.shape[2]), turned], axis=1)
    beams = lax.dot_general(flat.astype(jnp.float32), paired.astype(jnp.float32), (((0,), (0,)), ((), ())), preferred_element_type=jnp.float32)
    return jnp.sum(beams * beams, axis=1)

def covariance_term(steering, weights):
    scaled = (steering.astype(jnp.float32) * weights[None, None, :]).astype(jnp.bfloat16)
    upper = jnp.concatenate([scaled[0], scaled[1]], axis=1)
    lower = jnp.concatenate([scaled[1], -scaled[0]], axis=1)
    right = jnp.concatenate([steering[0], steering[1]], axis=1)
    left = jnp.concatenate([upper, lower], axis=0)
    return lax.dot_general(left.astype(jnp.float32), right.astype(jnp.float32), (((1,), (1,)), ((), ())), preferred_element_type=jnp.float32)

def factor(covariance):
    half = covariance.shape[1]
    real_part = covariance[:half]
    imag_part = covariance[half:]
    loading = jnp.trace(real_part) / half
    embedded = jnp.concatenate([jnp.concatenate([real_part, -imag_part], axis=1), jnp.concatenate([imag_part, real_part], axis=1)], axis=0)
    embedded = embedded + loading * jnp.eye(2 * half, dtype=jnp.float32)
    return jnp.linalg.cholesky(embedded)

def reference(cube, select, phases, jitter):
    picked = jnp.take(cube, select, axis=2)
    groups = N_ANG * N_SNAP
    width = K // groups
    indices = jnp.arange(groups, dtype=jnp.int32)

    def block_of(index):
        return steering_block(index * width + jnp.arange(width, dtype=jnp.int32), phases, jitter, RX)

    def all_energy(samples):

        def one_block(index):
            return beam_power(block_of(index), samples)
        return lax.map(one_block, indices).reshape(K)
    powers = all_energy(picked) / (SNAPS * M * M)
    right_side = picked.reshape(2 * M, SNAPS).astype(jnp.float32)
    for iteration in range(ITERS):

        def add_term(total, index):
            weights = lax.dynamic_slice_in_dim(powers, index * width, width, 0)
            return (total + covariance_term(block_of(index), weights), None)
        covariance, leftover = lax.scan(add_term, jnp.zeros((2 * M, M), jnp.float32), indices)
        lower_factor = factor(covariance)
        middle = jax.scipy.linalg.solve_triangular(lower_factor, right_side, lower=True)
        solved = jax.scipy.linalg.solve_triangular(lower_factor, middle, lower=True, trans=1)
        filtered = solved.astype(jnp.bfloat16).reshape(2, M, SNAPS)

        def block_norms(index):
            columns = block_of(index).reshape(2 * M, width).astype(jnp.float32)
            whitened = jax.scipy.linalg.solve_triangular(lower_factor, columns, lower=True)
            return jnp.sum(whitened * whitened, axis=0)
        norms = lax.map(block_norms, indices).reshape(K)
        powers = all_energy(filtered) / (SNAPS * norms * norms)
    return powers
```

```python
import functools
import math

import jax
import jax.numpy as jnp
from jax import lax
from jax.experimental import pallas as pl
from jax.experimental.pallas import tpu as pltpu
from jax.sharding import PartitionSpec as P

RX = 32
GU = 128
GV = 128
Q = 64
ITERS = 3
K = GU * GV

TILE = 128
PAIR = 2 * TILE
F32 = jnp.float32
BF16 = jnp.bfloat16


def nt_dot(left, right):
    return lax.dot_general(left, right, (((1,), (1,)), ((), ())), preferred_element_type=F32)


def dot(left, right):
    return jnp.dot(left, right, preferred_element_type=F32)


def split(x):
    high = x.astype(BF16)
    return high, (x - high.astype(F32)).astype(BF16)


def dot3(left, right):
    left_high, left_low = split(left)
    right_high, right_low = split(right)
    return dot(left_high, right_high) + (dot(left_low, right_high) + dot(left_high, right_low))


def block_pairs(blocks):
    first, second = [], []
    for a in range(blocks):
        for b in range(a, blocks):
            first.append((a, b))
    half = (len(first) + 1) // 2
    first, second = first[:half], first[half:]
    second = [(b, a) for a, b in second]
    while len(second) < half:
        second.append(second[-1])
    return first, second


def complex_block(gram):
    real = gram[:TILE, :TILE] + gram[TILE:, TILE:]
    imag = gram[TILE:, :TILE] - gram[:TILE, TILE:]
    return real, imag


def steering_kernel(steps, real_ref, imag_ref, turn_real_ref, turn_imag_ref, out_ref):
    real, imag = real_ref[0], imag_ref[0]
    turn_real, turn_imag = turn_real_ref[...], turn_imag_ref[...]
    for step in range(steps):
        if step:
            real, imag = real * turn_real - imag * turn_imag, real * turn_imag + imag * turn_real
        columns = slice(step * GV, (step + 1) * GV)
        out_ref[0, :TILE, columns] = real.astype(BF16)
        out_ref[0, TILE:, columns] = imag.astype(BF16)


def all_steering(phases, jitter):
    channels = phases.shape[0] * RX
    blocks = channels // TILE
    steps = 8
    starts = GU // steps
    channel = jnp.arange(channels, dtype=jnp.int32)
    position_x = (channel % RX).astype(F32) + jitter[0]
    position_y = (channel // RX).astype(F32) + jitter[1]
    offsets = jnp.broadcast_to(phases[:, None], (phases.shape[0], RX)).reshape(channels).astype(F32)
    row_angle = (2 * steps * jnp.arange(starts, dtype=jnp.int32) - GU).astype(F32) / GU
    col_angle = (2 * jnp.arange(GV, dtype=jnp.int32) - GV).astype(F32) / GV
    angle = math.pi * (
        position_x[None, :, None] * row_angle[:, None, None] + position_y[None, :, None] * col_angle[None, None, :]
    )
    angle = angle + 2.0 * math.pi / Q * offsets[None, :, None]
    turn = jnp.broadcast_to((math.pi * 2.0 / GU) * position_x[:, None], (channels, GV))
    start_spec = pl.BlockSpec((1, TILE, GV), lambda b, s: (s, b, 0))
    turn_spec = pl.BlockSpec((TILE, GV), lambda b, s: (b, 0))
    return pl.pallas_call(
        functools.partial(steering_kernel, steps),
        grid=(blocks, starts),
        in_specs=[start_spec, start_spec, turn_spec, turn_spec],
        out_specs=pl.BlockSpec((1, PAIR, steps * GV), lambda b, s: (b, 0, s)),
        out_shape=jax.ShapeDtypeStruct((blocks, PAIR, K), BF16),
        name="steering",
    )(jnp.cos(angle), jnp.sin(angle), jnp.cos(turn), jnp.sin(turn))


def sample_kernel(pairs, cube_ref, select_ref, out_ref):
    cells = cube_ref.shape[2]
    shots = select_ref.shape[1]
    wanted = jnp.broadcast_to(select_ref[...], (cells, shots))
    chosen = (lax.broadcasted_iota(jnp.int32, (cells, shots), 0) == wanted).astype(F32).astype(BF16)
    blocks = cube_ref.shape[1] // TILE
    picked = []
    for block in range(blocks):
        rows = slice(block * TILE, (block + 1) * TILE)
        both = jnp.concatenate([cube_ref[0, rows, :], cube_ref[1, rows, :]], axis=0)
        picked.append(dot(both, chosen).astype(BF16))
    for index, (a, b) in enumerate(pairs):
        real, imag = complex_block(nt_dot(picked[a], picked[b]))
        out_ref[2 * index] = real
        out_ref[2 * index + 1] = imag


def sample_terms(cube, select, pairs):
    return pl.pallas_call(
        functools.partial(sample_kernel, pairs),
        out_shape=jax.ShapeDtypeStruct((2 * len(pairs), TILE, TILE), F32),
        name="sample",
    )(cube, select[None, :])


def swap(x, axis, mask):
    size = lax.axis_size(axis)
    return lax.ppermute(x, axis, [(i, i ^ mask) for i in range(size)])


def sum_over(x, axis):
    size = lax.axis_size(axis)
    index = lax.axis_index(axis)
    masks = [1 << i for i in range(size.bit_length() - 1)]
    for mask in masks:
        half = x.shape[0] // 2
        high = (index // mask) % 2
        keep = lax.dynamic_slice_in_dim(x, high * half, half, 0)
        give = lax.dynamic_slice_in_dim(x, (1 - high) * half, half, 0)
        x = keep + swap(give, axis, mask)
    for mask in reversed(masks):
        high = (index // mask) % 2
        other = swap(x, axis, mask)
        x = jnp.where(high == 0, jnp.concatenate([x, other]), jnp.concatenate([other, x]))
    return x


def gather_relative(x):
    snap, ang = lax.axis_size("snap"), lax.axis_size("ang")
    if snap > 1:
        x = jnp.concatenate([x, swap(x, "snap", 1)], axis=0)
    x = jnp.concatenate([x] + [swap(x, "snap", m) for m in range(2, snap, 2)], axis=0)
    return jnp.concatenate([x] + [swap(x, "ang", m) for m in range(1, ang)], axis=0)


def covariance_kernel(table_ref, steering_ref, powers_ref, out_ref, total):
    step = pl.program_id(0)
    count = total.shape[0]

    @pl.when(step == 0)
    def _():
        total[...] = jnp.zeros_like(total)

    weights = powers_ref[0]
    for n in range(count):
        a, b = table_ref[1 + 2 * n], table_ref[2 + 2 * n]
        scaled = (steering_ref[a].astype(F32) * weights).astype(BF16)
        total[n] += nt_dot(scaled, steering_ref[b])

    @pl.when(step == pl.num_programs(0) - 1)
    def _():
        for n in range(count):
            real, imag = complex_block(total[n])
            out_ref[2 * n] = real
            out_ref[2 * n + 1] = imag


def covariance_half(table, steering, powers, count):
    blocks = steering.shape[0]
    devices, owned = powers.shape
    grid_spec = pltpu.PrefetchScalarGridSpec(
        num_scalar_prefetch=1,
        grid=(devices,),
        in_specs=[
            pl.BlockSpec((blocks, PAIR, owned), lambda s, t: (0, 0, s ^ t[0])),
            pl.BlockSpec((1, 1, owned), lambda s, t: (s, 0, 0)),
        ],
        out_specs=pl.BlockSpec((2 * count, TILE, TILE), lambda s, t: (0, 0, 0)),
        scratch_shapes=[pltpu.VMEM((count, PAIR, PAIR), F32)],
    )
    return pl.pallas_call(
        covariance_kernel,
        grid_spec=grid_spec,
        out_shape=jax.ShapeDtypeStruct((2 * count, TILE, TILE), F32),
        name="covariance",
    )(table, steering, powers[:, None, :])


def embed(store, i, j, real, imag):
    top, left = i * PAIR, j * PAIR
    store(slice(top, top + TILE), slice(left, left + TILE), real)
    store(slice(top, top + TILE), slice(left + TILE, left + PAIR), -imag)
    store(slice(top + TILE, top + PAIR), slice(left, left + TILE), imag)
    store(slice(top + TILE, top + PAIR), slice(left + TILE, left + PAIR), real)


def first_kernel(pairs, scale, me_ref, sample_ref, steering_ref, high_ref, low_ref, out_ref):
    def store(rows, columns, value):
        high, low = split(value)
        high_ref[rows, columns] = high
        low_ref[rows, columns] = low

    for index, (a, b) in enumerate(pairs):
        real, imag = sample_ref[2 * index], sample_ref[2 * index + 1]
        embed(store, a, b, real, imag)
        if a != b:
            embed(store, b, a, real.T, -imag.T)
    vectors = steering_ref[...].reshape(steering_ref.shape[0] * PAIR, steering_ref.shape[2])
    turned = dot(high_ref[...], vectors) + dot(low_ref[...], vectors)
    out_ref[...] = jnp.sum(turned * vectors.astype(F32), axis=0, keepdims=True) / scale


def first_powers(me, sample, steering, owned, pairs, scale):
    blocks = steering.shape[0]
    order = blocks * PAIR
    whole = lambda *shape: pl.BlockSpec(shape, lambda s, m: (0,) * len(shape))
    grid_spec = pltpu.PrefetchScalarGridSpec(
        num_scalar_prefetch=1,
        grid=(1,),
        in_specs=[whole(*sample.shape), pl.BlockSpec((blocks, PAIR, owned), lambda s, m: (0, 0, m[0]))],
        out_specs=[whole(order, order), whole(order, order), whole(1, owned)],
    )
    return pl.pallas_call(
        functools.partial(first_kernel, pairs, scale),
        grid_spec=grid_spec,
        out_shape=[
            jax.ShapeDtypeStruct((order, order), BF16),
            jax.ShapeDtypeStruct((order, order), BF16),
            jax.ShapeDtypeStruct((1, owned), F32),
        ],
        name="first",
    )(me, sample, steering)


def invert_tile(real, imag):
    order = real.shape[0]
    lane = lax.broadcasted_iota(jnp.int32, (1, order), 1)
    sublane = lax.broadcasted_iota(jnp.int32, (8, order), 0)

    def group(_, carry):
        real, imag = carry
        for j in range(8):
            inverse = 1.0 / real[j : j + 1, j : j + 1]
            hit = lane == j
            row_real = jnp.where(hit, -inverse, real[j : j + 1, :] * inverse)
            row_imag = jnp.where(hit, 0.0, imag[j : j + 1, :] * inverse)
            col_real, col_imag = real[:, j : j + 1], imag[:, j : j + 1]
            new_real = jnp.where(hit, 0.0, real) - (col_real * row_real - col_imag * row_imag)
            new_imag = jnp.where(hit, 0.0, imag) - (col_real * row_imag + col_imag * row_real)
            here = sublane == j
            top_real = jnp.where(here, row_real, new_real[:8])
            top_imag = jnp.where(here, row_imag, new_imag[:8])
            real = jnp.concatenate([top_real, new_real[8:]], axis=0)
            imag = jnp.concatenate([top_imag, new_imag[8:]], axis=0)
        real = pltpu.roll(jnp.concatenate([real[8:], real[:8]], axis=0), order - 8, 1)
        imag = pltpu.roll(jnp.concatenate([imag[8:], imag[:8]], axis=0), order - 8, 1)
        return real, imag

    real, imag = lax.fori_loop(0, order // 8, group, (real, imag))
    return -real, -imag


def step_kernel(
    pairs, shots, where_ref, mine_ref, other_ref, steering_ref, high_ref, low_ref, out_ref, matrix, inv_high, inv_low
):
    order = matrix.shape[0]
    blocks = order // TILE
    half = len(pairs[0])

    def rows(i):
        return slice(i * TILE, (i + 1) * TILE)

    def cols(i, part):
        return slice(part * order + i * TILE, part * order + (i + 1) * TILE)

    def put(group, ref):
        for index, (a, b) in enumerate(pairs[group]):
            real, imag = ref[2 * index], ref[2 * index + 1]
            if a == b:
                matrix[rows(a), cols(a, 0)] = 0.5 * (real + real.T)
                matrix[rows(a), cols(a, 1)] = 0.5 * (imag - imag.T)
            else:
                matrix[rows(a), cols(b, 0)] = real
                matrix[rows(a), cols(b, 1)] = imag
                matrix[rows(b), cols(a, 0)] = real.T
                matrix[rows(b), cols(a, 1)] = -imag.T

    @pl.when(where_ref[1] == 0)
    def _():
        put(0, mine_ref)
        put(1, other_ref)

    @pl.when(where_ref[1] != 0)
    def _():
        put(1, mine_ref)
        put(0, other_ref)

    diagonal = lax.broadcasted_iota(jnp.int32, (TILE, TILE), 0) == lax.broadcasted_iota(jnp.int32, (TILE, TILE), 1)
    trace = jnp.zeros((1, 1), F32)
    for i in range(blocks):
        kept = jnp.where(diagonal, matrix[rows(i), cols(i, 0)], 0.0)
        trace = trace + jnp.sum(jnp.sum(kept, axis=0, keepdims=True), axis=1, keepdims=True)
    loading = trace / order
    for i in range(blocks):
        matrix[rows(i), cols(i, 0)] += jnp.where(diagonal, loading, 0.0)

    unit = jnp.where(diagonal, 1.0, 0.0)
    nothing = jnp.zeros((TILE, TILE), F32)
    for k in range(blocks):
        real, imag = invert_tile(matrix[rows(k), cols(k, 0)], matrix[rows(k), cols(k, 1)])
        column = jnp.concatenate([matrix[:, cols(k, 0)], matrix[:, cols(k, 1)]], axis=1)
        matrix[rows(k), cols(k, 0)] = unit
        matrix[rows(k), cols(k, 1)] = nothing
        row_real, row_imag = matrix[rows(k), :order], matrix[rows(k), order:]
        panel = jnp.concatenate([row_real, row_imag], axis=1)
        turned = jnp.concatenate([-row_imag, row_real], axis=1)
        row = dot3(jnp.concatenate([real, imag], axis=1), jnp.concatenate([panel, turned], axis=0))
        row_turned = jnp.concatenate([-row[:, order:], row[:, :order]], axis=1)
        tall = jnp.concatenate([row, row_turned], axis=0)
        for i in range(blocks):
            if i == k:
                matrix[rows(k), :] = row
            else:
                matrix[rows(i), cols(k, 0)] = nothing
                matrix[rows(i), cols(k, 1)] = nothing
                matrix[rows(i), :] -= dot3(column[rows(i)], tall)

    def store(at_rows, at_columns, value):
        high, low = split(value)
        inv_high[at_rows, at_columns] = high
        inv_low[at_rows, at_columns] = low

    weights = []
    for i in range(blocks):
        for j in range(blocks):
            real, imag = matrix[rows(i), cols(j, 0)], matrix[rows(i), cols(j, 1)]
            if i == j:
                weight = jnp.sum(jnp.where(diagonal, real, 0.0), axis=1, keepdims=True)
                weights += [weight, weight]
                real = jnp.where(diagonal, 0.0, real)
            embed(store, i, j, real, imag)
    vectors = steering_ref[...].reshape(2 * order, steering_ref.shape[2])
    wide = vectors.astype(F32)
    solved = dot(inv_high[...], vectors) + dot(inv_low[...], vectors) + jnp.concatenate(weights, axis=0) * wide
    norms = jnp.sum(solved * wide, axis=0, keepdims=True)
    solved_high, solved_low = split(solved)
    turned = dot(high_ref[...], solved_high) + (dot(low_ref[...], solved_high) + dot(high_ref[...], solved_low))
    energy = jnp.sum(turned * solved, axis=0, keepdims=True)
    out_ref[...] = energy / (shots * norms * norms)


def next_powers(where, mine, other, steering, high, low, owned, pairs, shots):
    blocks = steering.shape[0]
    order = blocks * TILE
    whole = lambda *shape: pl.BlockSpec(shape, lambda s, m: (0,) * len(shape))
    grid_spec = pltpu.PrefetchScalarGridSpec(
        num_scalar_prefetch=1,
        grid=(1,),
        in_specs=[
            whole(*mine.shape),
            whole(*other.shape),
            pl.BlockSpec((blocks, PAIR, owned), lambda s, m: (0, 0, m[0])),
            whole(2 * order, 2 * order),
            whole(2 * order, 2 * order),
        ],
        out_specs=whole(1, owned),
        scratch_shapes=[
            pltpu.VMEM((order, 2 * order), F32),
            pltpu.VMEM((2 * order, 2 * order), BF16),
            pltpu.VMEM((2 * order, 2 * order), BF16),
        ],
    )
    return pl.pallas_call(
        functools.partial(step_kernel, pairs, shots),
        grid_spec=grid_spec,
        out_shape=jax.ShapeDtypeStruct((1, owned), F32),
        name="step",
        compiler_params=pltpu.CompilerParams(vmem_limit_bytes=56 * 1024 * 1024),
    )(where, mine, other, steering, high, low)


def shards(cube, select, phases, jitter):
    snap_count, ang_count = lax.axis_size("snap"), lax.axis_size("ang")
    snap_index, ang_index = lax.axis_index("snap"), lax.axis_index("ang")
    channels = cube.shape[1]
    shots = select.shape[0] * snap_count
    owned = K // (ang_count * snap_count)
    pairs = block_pairs(channels // TILE)
    count = len(pairs[0])
    core = snap_index % 2
    me = (ang_index * snap_count + snap_index).astype(jnp.int32)
    where = jnp.stack([me, core.astype(jnp.int32)])
    flat = [jnp.array([x for pair in group for x in pair], jnp.int32) for group in pairs]
    table = jnp.concatenate([me[None], jnp.where(core == 0, flat[0], flat[1])])

    steering = all_steering(phases, jitter)
    every = [(a, b) for a in range(channels // TILE) for b in range(a + 1)]
    sample = sample_terms(cube, select - snap_index * cube.shape[2], every)
    rows = sample.shape[0] * TILE
    sample = sum_over(sample.reshape(rows, TILE), "snap").reshape(sample.shape)
    high, low, powers = first_powers(me[None], sample, steering, owned, every, float(shots * channels * channels))
    for _ in range(ITERS):
        mine = covariance_half(table, steering, gather_relative(powers), count)
        other = swap(mine, "snap", 1)
        powers = next_powers(where, mine, other, steering, high, low, owned, pairs, float(shots))
    return powers[0]


def solution(mesh):
    return jax.shard_map(
        shards,
        mesh=mesh,
        in_specs=(P(None, None, "snap"), P("snap"), P(), P()),
        out_specs=P(("ang", "snap")),
        check_vma=False,
    )
```

```python
import functools
import math

import jax
import jax.numpy as jnp
from jax import lax
from jax.experimental import pallas as pl
from jax.experimental.pallas import tpu as pltpu
from jax.sharding import PartitionSpec as P

RX = 32
GU = 128
GV = 128
Q = 64
ITERS = 3
K = GU * GV

TILE = 128
PAIR = 2 * TILE
WIDTH = 2048
PANEL = 16
F32 = jnp.float32
BF16 = jnp.bfloat16


def nt_dot(left, right):
    return lax.dot_general(left, right, (((1,), (1,)), ((), ())), preferred_element_type=F32)


def dot(left, right):
    return jnp.dot(left, right, preferred_element_type=F32)


def split(x):
    high = x.astype(BF16)
    return high, (x - high.astype(F32)).astype(BF16)


def dot3(left, right):
    left_high, left_low = split(left)
    right_high, right_low = split(right)
    return dot(left_high, right_high) + (dot(left_low, right_high) + dot(left_high, right_low))


def block_groups(blocks):
    groups = ([], [])
    for a in range(blocks):
        reach = blocks // 2 + (1 if a < blocks // 2 or blocks % 2 else 0)
        groups[a % 2].append((a, [(a + r) % blocks for r in range(reach)]))
    return groups


def group_pairs(group):
    return [(a, b) for a, partners in group for b in partners]


def complex_block(gram):
    real = gram[:TILE, :TILE] + gram[TILE:, TILE:]
    imag = gram[TILE:, :TILE] - gram[:TILE, TILE:]
    return real, imag


def steering_kernel(steps, start_real_ref, start_imag_ref, col_real_ref, col_imag_ref, turn_real_ref, turn_imag_ref, out_ref):
    chunk = pl.program_id(0)
    part = TILE // 2
    lane = lax.broadcasted_iota(jnp.int32, (part, GV), 1)
    for half in range(2):
        rows = slice(half * part, (half + 1) * part)
        here = lane == chunk
        start_real = jnp.sum(jnp.where(here, start_real_ref[rows, :], 0.0), axis=1, keepdims=True)
        start_imag = jnp.sum(jnp.where(here, start_imag_ref[rows, :], 0.0), axis=1, keepdims=True)
        col_real, col_imag = col_real_ref[rows, :], col_imag_ref[rows, :]
        real = col_real * start_real - col_imag * start_imag
        imag = col_real * start_imag + col_imag * start_real
        turn_real, turn_imag = turn_real_ref[rows, :], turn_imag_ref[rows, :]
        for step in range(steps):
            if step:
                real, imag = real * turn_real - imag * turn_imag, real * turn_imag + imag * turn_real
            columns = slice(step * GV, (step + 1) * GV)
            out_ref[0, 0, rows, columns] = real.astype(BF16)
            out_ref[0, 0, slice(TILE + half * part, TILE + (half + 1) * part), columns] = imag.astype(BF16)


def all_steering(phases, jitter, width):
    channels = phases.shape[0] * RX
    blocks = channels // TILE
    steps = width // GV
    chunks = K // width
    channel = jnp.arange(channels, dtype=jnp.int32)
    position_x = (channel % RX).astype(F32) + jitter[0]
    position_y = (channel // RX).astype(F32) + jitter[1]
    offsets = jnp.broadcast_to(phases[:, None], (phases.shape[0], RX)).reshape(channels).astype(F32)
    lane = jnp.arange(GV, dtype=jnp.int32)
    row_angle = (2 * steps * lane - GU).astype(F32) / GU
    col_angle = (2 * lane - GV).astype(F32) / GV
    start = math.pi * (position_x[:, None] * row_angle[None, :])
    col = math.pi * (position_y[:, None] * col_angle[None, :]) + 2.0 * math.pi / Q * offsets[:, None]
    turn = jnp.broadcast_to((math.pi * 2.0 / GU) * position_x[:, None], (channels, GV))
    angles = jnp.stack([start, col, turn])
    real, imag = jnp.cos(angles), jnp.sin(angles)
    spec = pl.BlockSpec((TILE, GV), lambda s, b: (b, 0))
    return pl.pallas_call(
        functools.partial(steering_kernel, steps),
        grid=(chunks, blocks),
        in_specs=[spec] * 6,
        out_specs=pl.BlockSpec((1, 1, PAIR, width), lambda s, b: (s, b, 0, 0)),
        out_shape=jax.ShapeDtypeStruct((chunks, blocks, PAIR, width), BF16),
        name="steering",
    )(real[0], imag[0], real[1], imag[1], real[2], imag[2])


def own_block(shape, owned):
    per = shape[3] // owned
    return pl.BlockSpec((1, shape[1], PAIR, owned), lambda s, m: (m[0] // per, 0, 0, m[0] % per))


def sample_kernel(pairs, cube_ref, select_ref, out_ref):
    cells = cube_ref.shape[2]
    shots = select_ref.shape[1]
    wanted = jnp.broadcast_to(select_ref[...], (cells, shots))
    chosen = (lax.broadcasted_iota(jnp.int32, (cells, shots), 0) == wanted).astype(F32).astype(BF16)
    blocks = cube_ref.shape[1] // TILE
    picked = []
    for block in range(blocks):
        rows = slice(block * TILE, (block + 1) * TILE)
        both = jnp.concatenate([cube_ref[0, rows, :], cube_ref[1, rows, :]], axis=0)
        picked.append(dot(both, chosen).astype(BF16))
    for index, (a, b) in enumerate(pairs):
        real, imag = complex_block(nt_dot(picked[a], picked[b]))
        out_ref[2 * index] = real
        out_ref[2 * index + 1] = imag


def sample_terms(cube, select, pairs):
    return pl.pallas_call(
        functools.partial(sample_kernel, pairs),
        out_shape=jax.ShapeDtypeStruct((2 * len(pairs), TILE, TILE), F32),
        name="sample",
    )(cube, select[None, :])


def swap(x, axis, mask):
    size = lax.axis_size(axis)
    return lax.ppermute(x, axis, [(i, i ^ mask) for i in range(size)])


def sum_over(x, axis):
    size = lax.axis_size(axis)
    index = lax.axis_index(axis)
    masks = [1 << i for i in range(size.bit_length() - 1)]
    for mask in masks:
        half = x.shape[0] // 2
        high = (index // mask) % 2
        keep = lax.dynamic_slice_in_dim(x, high * half, half, 0)
        give = lax.dynamic_slice_in_dim(x, (1 - high) * half, half, 0)
        x = keep + swap(give, axis, mask)
    for mask in reversed(masks):
        high = (index // mask) % 2
        other = swap(x, axis, mask)
        x = jnp.where(high == 0, jnp.concatenate([x, other]), jnp.concatenate([other, x]))
    return x


def gather_relative(x):
    snap, ang = lax.axis_size("snap"), lax.axis_size("ang")
    if snap > 1:
        x = jnp.concatenate([x, swap(x, "snap", 1)], axis=0)
    x = jnp.concatenate([x] + [swap(x, "snap", m) for m in range(2, snap, 2)], axis=0)
    return jnp.concatenate([x] + [swap(x, "ang", m) for m in range(1, ang)], axis=0)


def covariance_kernel(slots, table_ref, steering_ref, powers_ref, out_ref, scaled, total):
    step = pl.program_id(0)
    owned = powers_ref.shape[1]
    per = steering_ref.shape[3] // owned
    low = table_ref[0] % per

    @pl.when(step == 0)
    def _():
        total[...] = jnp.zeros_like(total)

    weights = jnp.concatenate([powers_ref[pl.ds(step * per + (q ^ low), 1), :] for q in range(per)], axis=1)
    used = max(slots) + 1
    for slot in range(used):
        scaled[slot] = (steering_ref[0, table_ref[1 + slot]].astype(F32) * weights).astype(BF16)
    for n, slot in enumerate(slots):
        total[n] += nt_dot(scaled[slot], steering_ref[0, table_ref[1 + used + n]])

    @pl.when(step == pl.num_programs(0) - 1)
    def _():
        for n in range(len(slots)):
            real, imag = complex_block(total[n])
            out_ref[2 * n] = real
            out_ref[2 * n + 1] = imag


def covariance_half(table, steering, powers, slots):
    chunks, blocks, pair, width = steering.shape
    devices, owned = powers.shape
    per = width // owned
    count = len(slots)
    grid_spec = pltpu.PrefetchScalarGridSpec(
        num_scalar_prefetch=1,
        grid=(chunks,),
        in_specs=[
            pl.BlockSpec((1, blocks, pair, width), lambda s, t: (s ^ (t[0] // per), 0, 0, 0)),
            pl.BlockSpec((devices, owned), lambda s, t: (0, 0)),
        ],
        out_specs=pl.BlockSpec((2 * count, TILE, TILE), lambda s, t: (0, 0, 0)),
        scratch_shapes=[
            pltpu.VMEM((max(slots) + 1, PAIR, width), BF16),
            pltpu.VMEM((count, PAIR, PAIR), F32),
        ],
    )
    return pl.pallas_call(
        functools.partial(covariance_kernel, slots),
        grid_spec=grid_spec,
        out_shape=jax.ShapeDtypeStruct((2 * count, TILE, TILE), F32),
        name="covariance",
    )(table, steering, powers)


def embed(store, i, j, real, imag):
    top, left = i * PAIR, j * PAIR
    store(slice(top, top + TILE), slice(left, left + TILE), real)
    store(slice(top, top + TILE), slice(left + TILE, left + PAIR), -imag)
    store(slice(top + TILE, top + PAIR), slice(left, left + TILE), imag)
    store(slice(top + TILE, top + PAIR), slice(left + TILE, left + PAIR), real)


def first_kernel(pairs, scale, me_ref, sample_ref, steering_ref, high_ref, low_ref, out_ref):
    def store(rows, columns, value):
        high, low = split(value)
        high_ref[rows, columns] = high
        low_ref[rows, columns] = low

    for index, (a, b) in enumerate(pairs):
        real, imag = sample_ref[2 * index], sample_ref[2 * index + 1]
        embed(store, a, b, real, imag)
        if a != b:
            embed(store, b, a, real.T, -imag.T)
    vectors = steering_ref[0].reshape(steering_ref.shape[1] * PAIR, steering_ref.shape[3])
    turned = dot(high_ref[...], vectors) + dot(low_ref[...], vectors)
    out_ref[...] = jnp.sum(turned * vectors.astype(F32), axis=0, keepdims=True) / scale


def first_powers(me, sample, steering, owned, pairs, scale):
    blocks = steering.shape[1]
    order = blocks * PAIR
    whole = lambda *shape: pl.BlockSpec(shape, lambda s, m: (0,) * len(shape))
    grid_spec = pltpu.PrefetchScalarGridSpec(
        num_scalar_prefetch=1,
        grid=(1,),
        in_specs=[whole(*sample.shape), own_block(steering.shape, owned)],
        out_specs=[whole(order, order), whole(order, order), whole(1, owned)],
    )
    return pl.pallas_call(
        functools.partial(first_kernel, pairs, scale),
        grid_spec=grid_spec,
        out_shape=[
            jax.ShapeDtypeStruct((order, order), BF16),
            jax.ShapeDtypeStruct((order, order), BF16),
            jax.ShapeDtypeStruct((1, owned), F32),
        ],
        name="first",
    )(me, sample, steering)


def take(x, index):
    return jnp.take_along_axis(x, index, axis=1, mode="promise_in_bounds")


def invert_tile(tile):
    lane_all = lax.broadcasted_iota(jnp.int32, (TILE, TILE), 1)
    lane = lax.broadcasted_iota(jnp.int32, (PANEL, TILE), 1)
    sublane = lax.broadcasted_iota(jnp.int32, (PANEL, TILE), 0)

    def panel(step, _):
        base = pl.multiple_of(step * PANEL, PANEL)
        real, imag = tile[:, :TILE], tile[:, TILE:]
        pattern = base + lane_all % PANEL
        sides = jnp.where((lane_all // PANEL) % 2 == 0, take(real, pattern), take(imag, pattern))
        high = sides.astype(BF16).astype(F32)
        left = jnp.where(lane_all // (2 * PANEL) == 1, sides - high, high).astype(BF16)
        row_real, row_imag = tile[pl.ds(base, PANEL), :TILE], tile[pl.ds(base, PANEL), TILE:]
        spots = [jnp.full((PANEL, TILE), base + j, jnp.int32) for j in range(PANEL)]
        col_real = [take(row_real, spot) for spot in spots]
        col_imag = [take(row_imag, spot) for spot in spots]
        for p in range(PANEL):
            own_real, own_imag = col_real[p], col_imag[p]
            inverse = 1.0 / own_real[p : p + 1, :]
            hit = lane == base + p
            here = sublane == p
            pivot_real = jnp.where(hit[:1], inverse, row_real[p : p + 1, :] * inverse)
            pivot_imag = jnp.where(hit[:1], 0.0, row_imag[p : p + 1, :] * inverse)
            rest_real = jnp.where(hit, 0.0, row_real) - (own_real * pivot_real - own_imag * pivot_imag)
            rest_imag = jnp.where(hit, 0.0, row_imag) - (own_real * pivot_imag + own_imag * pivot_real)
            row_real = jnp.where(here, pivot_real, rest_real)
            row_imag = jnp.where(here, pivot_imag, rest_imag)
            for j in range(p + 1, PANEL):
                pivot_real = col_real[j][p : p + 1, :] * inverse
                pivot_imag = col_imag[j][p : p + 1, :] * inverse
                rest_real = col_real[j] - (own_real * pivot_real - own_imag * pivot_imag)
                rest_imag = col_imag[j] - (own_real * pivot_imag + own_imag * pivot_real)
                col_real[j] = jnp.where(here, pivot_real, rest_real)
                col_imag[j] = jnp.where(here, pivot_imag, rest_imag)
        rows = jnp.concatenate([row_real, row_imag], axis=1)
        turned = jnp.concatenate([-row_imag, row_real], axis=1)
        both_high, both_low = split(jnp.concatenate([rows, turned], axis=0))
        right = jnp.concatenate([both_high, both_high, both_low, jnp.zeros_like(both_low)], axis=0)
        update = dot(left, right)
        inside = lane_all // PANEL == step
        tile[:, :TILE] = jnp.where(inside, 0.0, real) - update[:, :TILE]
        tile[:, TILE:] = jnp.where(inside, 0.0, imag) - update[:, TILE:]
        tile[pl.ds(base, PANEL), :] = rows
        return 0

    lax.fori_loop(0, TILE // PANEL, panel, 0)


def step_kernel(
    pairs, shots, where_ref, mine_ref, other_ref, steering_ref, high_ref, low_ref, out_ref, matrix, tile, inv_high, inv_low
):
    order = matrix.shape[0]
    blocks = order // TILE
    half = len(pairs[0])

    def rows(i):
        return slice(i * TILE, (i + 1) * TILE)

    def cols(i, part):
        return slice(part * order + i * TILE, part * order + (i + 1) * TILE)

    def put(group, ref):
        for index, (a, b) in enumerate(pairs[group]):
            real, imag = ref[2 * index], ref[2 * index + 1]
            if a == b:
                matrix[rows(a), cols(a, 0)] = 0.5 * (real + real.T)
                matrix[rows(a), cols(a, 1)] = 0.5 * (imag - imag.T)
            else:
                matrix[rows(a), cols(b, 0)] = real
                matrix[rows(a), cols(b, 1)] = imag
                matrix[rows(b), cols(a, 0)] = real.T
                matrix[rows(b), cols(a, 1)] = -imag.T

    @pl.when(where_ref[1] == 0)
    def _():
        put(0, mine_ref)
        put(1, other_ref)

    @pl.when(where_ref[1] != 0)
    def _():
        put(1, mine_ref)
        put(0, other_ref)

    diagonal = lax.broadcasted_iota(jnp.int32, (TILE, TILE), 0) == lax.broadcasted_iota(jnp.int32, (TILE, TILE), 1)
    trace = jnp.zeros((1, 1), F32)
    for i in range(blocks):
        kept = jnp.where(diagonal, matrix[rows(i), cols(i, 0)], 0.0)
        trace = trace + jnp.sum(jnp.sum(kept, axis=0, keepdims=True), axis=1, keepdims=True)
    loading = trace / order
    for i in range(blocks):
        matrix[rows(i), cols(i, 0)] += jnp.where(diagonal, loading, 0.0)

    unit = jnp.where(diagonal, 1.0, 0.0)
    nothing = jnp.zeros((TILE, TILE), F32)
    for k in range(blocks):
        tile[:, :TILE] = matrix[rows(k), cols(k, 0)]
        tile[:, TILE:] = matrix[rows(k), cols(k, 1)]
        invert_tile(tile)
        column = jnp.concatenate([matrix[:, cols(k, 0)], matrix[:, cols(k, 1)]], axis=1)
        matrix[rows(k), cols(k, 0)] = unit
        matrix[rows(k), cols(k, 1)] = nothing
        row_real, row_imag = matrix[rows(k), :order], matrix[rows(k), order:]
        panel = jnp.concatenate([row_real, row_imag], axis=1)
        turned = jnp.concatenate([-row_imag, row_real], axis=1)
        row = dot3(tile[...], jnp.concatenate([panel, turned], axis=0))
        row_turned = jnp.concatenate([-row[:, order:], row[:, :order]], axis=1)
        tall = jnp.concatenate([row, row_turned], axis=0)
        for i in range(blocks):
            if i == k:
                matrix[rows(k), :] = row
            else:
                matrix[rows(i), cols(k, 0)] = nothing
                matrix[rows(i), cols(k, 1)] = nothing
                matrix[rows(i), :] -= dot3(column[rows(i)], tall)

    def store(at_rows, at_columns, value):
        high, low = split(value)
        inv_high[at_rows, at_columns] = high
        inv_low[at_rows, at_columns] = low

    weights = []
    for i in range(blocks):
        for j in range(blocks):
            real, imag = matrix[rows(i), cols(j, 0)], matrix[rows(i), cols(j, 1)]
            if i == j:
                weight = jnp.sum(jnp.where(diagonal, real, 0.0), axis=1, keepdims=True)
                weights += [weight, weight]
                real = jnp.where(diagonal, 0.0, real)
            embed(store, i, j, real, imag)
    vectors = steering_ref[0].reshape(2 * order, steering_ref.shape[3])
    wide = vectors.astype(F32)
    solved = dot(inv_high[...], vectors) + dot(inv_low[...], vectors) + jnp.concatenate(weights, axis=0) * wide
    norms = jnp.sum(solved * wide, axis=0, keepdims=True)
    solved_high, solved_low = split(solved)
    turned = dot(high_ref[...], solved_high) + (dot(low_ref[...], solved_high) + dot(high_ref[...], solved_low))
    energy = jnp.sum(turned * solved, axis=0, keepdims=True)
    out_ref[...] = energy / (shots * norms * norms)


def next_powers(where, mine, other, steering, high, low, owned, pairs, shots):
    blocks = steering.shape[1]
    order = blocks * TILE
    whole = lambda *shape: pl.BlockSpec(shape, lambda s, m: (0,) * len(shape))
    grid_spec = pltpu.PrefetchScalarGridSpec(
        num_scalar_prefetch=1,
        grid=(1,),
        in_specs=[
            whole(*mine.shape),
            whole(*other.shape),
            own_block(steering.shape, owned),
            whole(2 * order, 2 * order),
            whole(2 * order, 2 * order),
        ],
        out_specs=whole(1, owned),
        scratch_shapes=[
            pltpu.VMEM((order, 2 * order), F32),
            pltpu.VMEM((TILE, PAIR), F32),
            pltpu.VMEM((2 * order, 2 * order), BF16),
            pltpu.VMEM((2 * order, 2 * order), BF16),
        ],
    )
    return pl.pallas_call(
        functools.partial(step_kernel, pairs, shots),
        grid_spec=grid_spec,
        out_shape=jax.ShapeDtypeStruct((1, owned), F32),
        name="step",
        compiler_params=pltpu.CompilerParams(vmem_limit_bytes=56 * 1024 * 1024),
    )(where, mine, other, steering, high, low)


def shards(cube, select, phases, jitter):
    snap_count, ang_count = lax.axis_size("snap"), lax.axis_size("ang")
    snap_index, ang_index = lax.axis_index("snap"), lax.axis_index("ang")
    channels = cube.shape[1]
    shots = select.shape[0] * snap_count
    owned = K // (ang_count * snap_count)
    groups = block_groups(channels // TILE)
    pairs = [group_pairs(group) for group in groups]
    slots = [slot for slot, (a, partners) in enumerate(groups[0]) for b in partners]
    core = snap_index % 2
    me = (ang_index * snap_count + snap_index).astype(jnp.int32)
    where = jnp.stack([me, core.astype(jnp.int32)])
    flat = [
        jnp.array([a for a, partners in group] + [b for a, b in group_pairs(group)], jnp.int32) for group in groups
    ]
    table = jnp.concatenate([me[None], jnp.where(core == 0, flat[0], flat[1])])

    steering = all_steering(phases, jitter, max(owned, WIDTH))
    every = [(a, b) for a in range(channels // TILE) for b in range(a + 1)]
    sample = sample_terms(cube, select - snap_index * cube.shape[2], every)
    rows = sample.shape[0] * TILE
    sample = sum_over(sample.reshape(rows, TILE), "snap").reshape(sample.shape)
    high, low, powers = first_powers(me[None], sample, steering, owned, every, float(shots * channels * channels))
    for _ in range(ITERS):
        mine = covariance_half(table, steering, gather_relative(powers), slots)
        other = swap(mine, "snap", 1)
        powers = next_powers(where, mine, other, steering, high, low, owned, pairs, float(shots))
    return powers[0]


def solution(mesh):
    return jax.shard_map(
        shards,
        mesh=mesh,
        in_specs=(P(None, None, "snap"), P("snap"), P(), P()),
        out_specs=P(("ang", "snap")),
        check_vma=False,
    )
```

```python
import functools
import math

import jax
import jax.numpy as jnp
from jax import lax
from jax.experimental import pallas as pl
from jax.experimental.pallas import tpu as pltpu
from jax.sharding import PartitionSpec as P


RX = 32
GU = 128
GV = 128
Q = 64
ITERS = 3
K = GU * GV

TILE = 128
PAIR = 2 * TILE
WIDTH = 2048
PANEL = 16
AHEAD = 6
F32 = jnp.float32
BF16 = jnp.bfloat16


def nt_dot(left, right):
    return lax.dot_general(left, right, (((1,), (1,)), ((), ())), preferred_element_type=F32)


def dot(left, right):
    return jnp.dot(left, right, preferred_element_type=F32)


def split(x):
    high = x.astype(BF16)
    return high, (x - high.astype(F32)).astype(BF16)


def dot3(left, right):
    left_high, left_low = split(left)
    right_high, right_low = split(right)
    return dot(left_high, right_high) + (dot(left_low, right_high) + dot(left_high, right_low))


def take(x, index):
    return jnp.take_along_axis(x, index, axis=1, mode="promise_in_bounds")


def cost(microseconds):
    return pl.CostEstimate(flops=microseconds * 10**9, bytes_accessed=microseconds * 3 * 10**6, transcendentals=0)


def block_groups(blocks):
    groups = ([], [])
    for a in range(blocks):
        reach = blocks // 2 + (1 if a < blocks // 2 or blocks % 2 else 0)
        groups[a % 2].append((a, [(a + r) % blocks for r in range(reach)]))
    return groups


def group_pairs(group):
    return [(a, b) for a, partners in group for b in partners]


def complex_block(gram):
    real = gram[:TILE, :TILE] + gram[TILE:, TILE:]
    imag = gram[TILE:, :TILE] - gram[:TILE, TILE:]
    return real, imag


def steering_kernel(steps, *refs):
    start_real, start_imag, col_real, col_imag, turn_real, turn_imag, out_ref = refs
    spot = jnp.full((TILE, GV), pl.program_id(0), jnp.int32)

    def block(b, _):
        rows = pl.ds(pl.multiple_of(b * TILE, TILE), TILE)
        first_real, first_imag = take(start_real[rows, :], spot), take(start_imag[rows, :], spot)
        across_real, across_imag = col_real[rows, :], col_imag[rows, :]
        real = across_real * first_real - across_imag * first_imag
        imag = across_real * first_imag + across_imag * first_real
        by_real, by_imag = turn_real[rows, :], turn_imag[rows, :]
        for step in range(steps):
            if step:
                real, imag = real * by_real - imag * by_imag, real * by_imag + imag * by_real
            columns = slice(step * GV, (step + 1) * GV)
            out_ref[0, b, :TILE, columns] = real.astype(BF16)
            out_ref[0, b, TILE:, columns] = imag.astype(BF16)
        return 0

    lax.fori_loop(0, out_ref.shape[1], block, 0)


def all_steering(phases, jitter, width):
    channels = phases.shape[0] * RX
    blocks = channels // TILE
    steps = width // GV
    chunks = K // width
    channel = jnp.arange(channels, dtype=jnp.int32)
    position_x = (channel % RX).astype(F32) + jitter[0]
    position_y = (channel // RX).astype(F32) + jitter[1]
    offsets = jnp.broadcast_to(phases[:, None], (phases.shape[0], RX)).reshape(channels).astype(F32)
    lane = jnp.arange(GV, dtype=jnp.int32)
    row_angle = (2 * steps * lane - GU).astype(F32) / GU
    col_angle = (2 * lane - GV).astype(F32) / GV
    start = math.pi * (position_x[:, None] * row_angle[None, :])
    col = math.pi * (position_y[:, None] * col_angle[None, :]) + 2.0 * math.pi / Q * offsets[:, None]
    turn = jnp.broadcast_to((math.pi * 2.0 / GU) * position_x[:, None], (channels, GV))
    angles = jnp.stack([start, col, turn])
    real, imag = jnp.cos(angles), jnp.sin(angles)
    spec = pl.BlockSpec((channels, GV), lambda s: (0, 0))
    return pl.pallas_call(
        functools.partial(steering_kernel, steps),
        grid=(chunks,),
        in_specs=[spec] * 6,
        out_specs=pl.BlockSpec((1, blocks, PAIR, width), lambda s: (s, 0, 0, 0)),
        out_shape=jax.ShapeDtypeStruct((chunks, blocks, PAIR, width), BF16),
        name="steering",
        cost_estimate=cost(17),
    )(real[0], imag[0], real[1], imag[1], real[2], imag[2])


def own_block(shape, owned):
    per = shape[3] // owned
    return pl.BlockSpec((1, shape[1], PAIR, owned), lambda s, m: (m[0] // per, 0, 0, m[0] % per))


def sample_kernel(pairs, cube_ref, select_ref, column_ref, gram_ref, shots_ref):
    cells = cube_ref.shape[2]
    shots = select_ref.shape[1]
    chosen = lax.broadcasted_iota(jnp.int32, (cells, shots), 0) == select_ref[...]
    chosen = jnp.where(chosen, 1.0, 0.0).astype(BF16)
    across = lax.broadcasted_iota(jnp.int32, (shots, cells), 1) == column_ref[...]
    across = jnp.where(across, 1.0, 0.0).astype(BF16)
    blocks = cube_ref.shape[1] // TILE
    picked = []
    for block in range(blocks):
        rows = slice(block * TILE, (block + 1) * TILE)
        both = jnp.concatenate([cube_ref[0, rows, :], cube_ref[1, rows, :]], axis=0)
        picked.append(dot(both, chosen).astype(BF16))
        flat = nt_dot(across, both)
        columns = slice(block * PAIR, (block + 1) * PAIR)
        shots_ref[:shots, columns] = flat.astype(BF16)
        shots_ref[shots:, columns] = jnp.concatenate([flat[:, TILE:], -flat[:, :TILE]], axis=1).astype(BF16)
    for index, (a, b) in enumerate(pairs):
        real, imag = complex_block(nt_dot(picked[a], picked[b]))
        gram_ref[2 * index] = real
        gram_ref[2 * index + 1] = imag


def sample_terms(cube, select, pairs):
    shots = select.shape[0]
    return pl.pallas_call(
        functools.partial(sample_kernel, pairs),
        out_shape=[
            jax.ShapeDtypeStruct((2 * len(pairs), TILE, TILE), F32),
            jax.ShapeDtypeStruct((2 * shots, 2 * cube.shape[1]), BF16),
        ],
        name="sample",
        cost_estimate=cost(4),
    )(cube, select[None, :], select[:, None])


def beam_kernel(where_ref, steering_ref, shots_ref, out_ref):
    vectors = steering_ref[0].reshape(shots_ref.shape[1], steering_ref.shape[3])
    beams = dot(shots_ref[...], vectors)
    out_ref[0] = jnp.sum(beams * beams, axis=0, keepdims=True)


def local_energy(where, steering, shots, owned):
    width = steering.shape[3]
    near = lax.axis_size("snap") * owned // width
    per = width // owned
    grid_spec = pltpu.PrefetchScalarGridSpec(
        num_scalar_prefetch=1,
        grid=(near,),
        in_specs=[
            pl.BlockSpec((1, *steering.shape[1:]), lambda s, m: (m[0] // (per * near) * near + s, 0, 0, 0)),
            pl.BlockSpec(shots.shape, lambda s, m: (0, 0)),
        ],
        out_specs=pl.BlockSpec((1, 1, width), lambda s, m: (s, 0, 0)),
    )
    return pl.pallas_call(
        beam_kernel,
        grid_spec=grid_spec,
        out_shape=jax.ShapeDtypeStruct((near, 1, width), F32),
        name="beams",
        cost_estimate=cost(5),
    )(where, steering, shots).reshape(near * per, owned)


def swap(x, axis, mask):
    size = lax.axis_size(axis)
    return lax.ppermute(x, axis, [(i, i ^ mask) for i in range(size)])


def halve(x, axis, bit):
    half = x.shape[0] // 2
    high = (lax.axis_index(axis) >> bit) % 2
    keep = lax.dynamic_slice_in_dim(x, high * half, half, 0)
    give = lax.dynamic_slice_in_dim(x, (1 - high) * half, half, 0)
    return keep + swap(give, axis, 1 << bit)


def piece_start(index, size, rows):
    start = 0
    for bit in range(size.bit_length() - 1):
        rows = rows // 2
        start = start + (index >> bit) % 2 * rows
    return start


def scatter_energy(rows):
    snap, index = lax.axis_size("snap"), lax.axis_index("snap")
    halves = rows.reshape(snap // 2, 2, rows.shape[1])
    core, high = index % 2, index // 2
    mine = lax.dynamic_index_in_dim(halves, core, 1, keepdims=False)
    give = lax.dynamic_index_in_dim(halves, 1 - core, 1, keepdims=False)
    both = mine + swap(give, "snap", 1)
    total = lax.dynamic_slice_in_dim(both, high, 1, 0)
    for m in range(1, snap // 2):
        total = total + swap(lax.dynamic_slice_in_dim(both, high ^ m, 1, 0), "snap", 2 * m)
    return total


def gather_relative(x):
    snap, ang = lax.axis_size("snap"), lax.axis_size("ang")
    x = jnp.concatenate([x, swap(x, "snap", 1)], axis=0)
    x = jnp.concatenate([x] + [swap(x, "snap", m) for m in range(2, snap, 2)], axis=0)
    return [x] + [swap(x, "ang", m) for m in range(1, ang)]


def covariance_kernel(slots, table_ref, steering_ref, *refs):
    *parts, out_ref, powers_ref, scaled, total = refs
    step = pl.program_id(0)
    owned = powers_ref.shape[1]
    per = steering_ref.shape[3] // owned
    low = table_ref[0] % per

    @pl.when(step == 0)
    def _():
        total[...] = jnp.zeros_like(total)
        for n, part in enumerate(parts):
            powers_ref[n * part.shape[0] : (n + 1) * part.shape[0], :] = part[...]

    weights = jnp.concatenate([powers_ref[pl.ds(step * per + (q ^ low), 1), :] for q in range(per)], axis=1)
    used = max(slots) + 1
    for slot in range(used):
        scaled[slot] = (steering_ref[0, table_ref[1 + slot]].astype(F32) * weights).astype(BF16)
    for n, slot in enumerate(slots):
        total[n] += nt_dot(scaled[slot], steering_ref[0, table_ref[1 + used + n]])

    @pl.when(step == pl.num_programs(0) - 1)
    def _():
        for n in range(len(slots)):
            real, imag = complex_block(total[n])
            out_ref[2 * n] = real
            out_ref[2 * n + 1] = imag


def covariance_half(table, steering, powers, slots):
    chunks, blocks, pair, width = steering.shape
    rows, owned = powers[0].shape
    per = width // owned
    count = len(slots)
    grid_spec = pltpu.PrefetchScalarGridSpec(
        num_scalar_prefetch=1,
        grid=(chunks,),
        in_specs=[
            pl.BlockSpec((1, blocks, pair, width), lambda s, t: (s ^ (t[0] // per), 0, 0, 0)),
        ]
        + [pl.BlockSpec((rows, owned), lambda s, t: (0, 0))] * len(powers),
        out_specs=pl.BlockSpec((2 * count, TILE, TILE), lambda s, t: (0, 0, 0)),
        scratch_shapes=[
            pltpu.VMEM((rows * len(powers), owned), F32),
            pltpu.VMEM((max(slots) + 1, PAIR, width), BF16),
            pltpu.VMEM((count, PAIR, PAIR), F32),
        ],
    )
    return pl.pallas_call(
        functools.partial(covariance_kernel, slots),
        grid_spec=grid_spec,
        out_shape=jax.ShapeDtypeStruct((2 * count, TILE, TILE), F32),
        name="covariance",
        cost_estimate=cost(17),
    )(table, steering, *powers)


def embed(store, i, j, real, imag):
    top, left = i * PAIR, j * PAIR
    store(slice(top, top + TILE), slice(left, left + TILE), real)
    store(slice(top, top + TILE), slice(left + TILE, left + PAIR), -imag)
    store(slice(top + TILE, top + PAIR), slice(left, left + TILE), imag)
    store(slice(top + TILE, top + PAIR), slice(left + TILE, left + PAIR), real)


def spread_kernel(pairs, size, where_ref, *refs):
    *parts, high_ref, low_ref, whole = refs
    half = size // 2
    piece = parts[0].shape[0] // half
    for core, part in enumerate(parts):
        for n in range(half):
            start = piece_start((where_ref[0] % size) ^ (2 * n + core), size, whole.shape[0])
            whole[pl.ds(pl.multiple_of(start, 8), piece), :] = part[n * piece : (n + 1) * piece, :]

    def store(rows, columns, value):
        high, low = split(value)
        high_ref[rows, columns] = high
        low_ref[rows, columns] = low

    for index, (a, b) in enumerate(pairs):
        real = whole[2 * index * TILE : (2 * index + 1) * TILE, :]
        imag = whole[(2 * index + 1) * TILE : (2 * index + 2) * TILE, :]
        embed(store, a, b, real, imag)
        if a != b:
            embed(store, b, a, real.T, -imag.T)


def spread(where, parts, pairs, order):
    size = lax.axis_size("snap")
    whole = lambda shape: pl.BlockSpec(shape, lambda s, m: (0, 0))
    return pl.pallas_call(
        functools.partial(spread_kernel, pairs, size),
        grid_spec=pltpu.PrefetchScalarGridSpec(
            num_scalar_prefetch=1,
            grid=(1,),
            in_specs=[whole(part.shape) for part in parts],
            out_specs=[whole((order, order))] * 2,
            scratch_shapes=[pltpu.VMEM((2 * len(pairs) * TILE, TILE), F32)],
        ),
        out_shape=[jax.ShapeDtypeStruct((order, order), BF16)] * 2,
        name="spread",
        cost_estimate=cost(3),
    )(where, *parts)


def invert_tile(tile):
    lane_all = lax.broadcasted_iota(jnp.int32, (TILE, TILE), 1)
    lane = lax.broadcasted_iota(jnp.int32, (PANEL, TILE), 1)
    sublane = lax.broadcasted_iota(jnp.int32, (PANEL, TILE), 0)

    def panel(step, _):
        base = pl.multiple_of(step * PANEL, PANEL)
        row_real, row_imag = tile[pl.ds(base, PANEL), :TILE], tile[pl.ds(base, PANEL), TILE:]

        def spread_column(j):
            spot = jnp.full((PANEL, TILE), base + j, jnp.int32)
            return take(row_real, spot), take(row_imag, spot)

        columns = {j: spread_column(j) for j in range(AHEAD)}
        real, imag = tile[:, :TILE], tile[:, TILE:]
        pattern = base + lane_all % PANEL
        sides = jnp.where((lane_all // PANEL) % 2 == 0, take(real, pattern), take(imag, pattern))
        high = sides.astype(BF16).astype(F32)
        left = jnp.where(lane_all // (2 * PANEL) == 1, sides - high, high).astype(BF16)
        for p in range(PANEL):
            if p + AHEAD < PANEL:
                columns[p + AHEAD] = spread_column(p + AHEAD)
            here = sublane == p
            hit = lane == base + p
            own_real, own_imag = columns.pop(p)
            inverse = 1.0 / own_real[p : p + 1, :]
            own_real = jnp.where(here, 1.0 - inverse, own_real * inverse)
            own_imag = jnp.where(here, 0.0, own_imag * inverse)

            def reduce(real, imag):
                pivot_real, pivot_imag = real[p : p + 1, :], imag[p : p + 1, :]
                return (
                    real - (own_real * pivot_real - own_imag * pivot_imag),
                    imag - (own_real * pivot_imag + own_imag * pivot_real),
                )

            row_real = jnp.where(hit, jnp.where(here, 1.0, 0.0), row_real)
            row_imag = jnp.where(hit, 0.0, row_imag)
            row_real, row_imag = reduce(row_real, row_imag)
            for j in columns:
                columns[j] = reduce(*columns[j])
        rows = jnp.concatenate([row_real, row_imag], axis=1)
        high, low = split(rows)
        turned_high = jnp.concatenate([-high[:, TILE:], high[:, :TILE]], axis=1)
        turned_low = jnp.concatenate([-low[:, TILE:], low[:, :TILE]], axis=1)
        right = [high, turned_high, high, turned_high, low, turned_low]
        right += [jnp.zeros_like(low)] * (TILE // PANEL - len(right))
        update = dot(left, jnp.concatenate(right, axis=0))
        inside = lane_all // PANEL == step
        tile[:, :TILE] = jnp.where(inside, 0.0, real) - update[:, :TILE]
        tile[:, TILE:] = jnp.where(inside, 0.0, imag) - update[:, TILE:]
        tile[pl.ds(base, PANEL), :] = rows
        return 0

    lax.fori_loop(0, TILE // PANEL, panel, 0)


def step_kernel(
    pairs, shots, where_ref, mine_ref, other_ref, steering_ref, high_ref, low_ref, out_ref, matrix, tile, inv_high, inv_low
):
    order = matrix.shape[0]
    blocks = order // TILE

    def rows(i):
        return slice(i * TILE, (i + 1) * TILE)

    def cols(i, part):
        return slice(part * order + i * TILE, part * order + (i + 1) * TILE)

    def put(group, ref):
        for index, (a, b) in enumerate(pairs[group]):
            real, imag = ref[2 * index], ref[2 * index + 1]
            if a == b:
                matrix[rows(a), cols(a, 0)] = 0.5 * (real + real.T)
                matrix[rows(a), cols(a, 1)] = 0.5 * (imag - imag.T)
            else:
                matrix[rows(a), cols(b, 0)] = real
                matrix[rows(a), cols(b, 1)] = imag
                matrix[rows(b), cols(a, 0)] = real.T
                matrix[rows(b), cols(a, 1)] = -imag.T

    @pl.when(where_ref[1] == 0)
    def _():
        put(0, mine_ref)
        put(1, other_ref)

    @pl.when(where_ref[1] != 0)
    def _():
        put(1, mine_ref)
        put(0, other_ref)

    diagonal = lax.broadcasted_iota(jnp.int32, (TILE, TILE), 0) == lax.broadcasted_iota(jnp.int32, (TILE, TILE), 1)
    trace = jnp.zeros((1, 1), F32)
    for i in range(blocks):
        kept = jnp.where(diagonal, matrix[rows(i), cols(i, 0)], 0.0)
        trace = trace + jnp.sum(jnp.sum(kept, axis=0, keepdims=True), axis=1, keepdims=True)
    matrix[...] = matrix[...] * (1.0 / trace)
    for i in range(blocks):
        matrix[rows(i), cols(i, 0)] += jnp.where(diagonal, 1.0 / order, 0.0)

    unit = jnp.where(diagonal, 1.0, 0.0)
    nothing = jnp.zeros((TILE, TILE), F32)
    for k in range(blocks):
        tile[:, :TILE] = matrix[rows(k), cols(k, 0)]
        tile[:, TILE:] = matrix[rows(k), cols(k, 1)]
        invert_tile(tile)
        column = jnp.concatenate([matrix[:, cols(k, 0)], matrix[:, cols(k, 1)]], axis=1)
        matrix[rows(k), cols(k, 0)] = unit
        matrix[rows(k), cols(k, 1)] = nothing
        row_real, row_imag = matrix[rows(k), :order], matrix[rows(k), order:]
        panel = jnp.concatenate([row_real, row_imag], axis=1)
        turned = jnp.concatenate([-row_imag, row_real], axis=1)
        row = dot3(tile[...], jnp.concatenate([panel, turned], axis=0))
        row_turned = jnp.concatenate([-row[:, order:], row[:, :order]], axis=1)
        tall = jnp.concatenate([row, row_turned], axis=0)
        for i in range(blocks):
            if i == k:
                matrix[rows(k), :] = row
            else:
                matrix[rows(i), cols(k, 0)] = nothing
                matrix[rows(i), cols(k, 1)] = nothing
                matrix[rows(i), :] -= dot3(column[rows(i)], tall)

    def store(at_rows, at_columns, value):
        high, low = split(value)
        inv_high[at_rows, at_columns] = high
        inv_low[at_rows, at_columns] = low

    weights = []
    for i in range(blocks):
        for j in range(blocks):
            real, imag = matrix[rows(i), cols(j, 0)], matrix[rows(i), cols(j, 1)]
            if i == j:
                weight = jnp.sum(jnp.where(diagonal, real, 0.0), axis=1, keepdims=True)
                weights += [weight, weight]
                real = jnp.where(diagonal, 0.0, real)
            embed(store, i, j, real, imag)
    vectors = steering_ref[0].reshape(2 * order, steering_ref.shape[3])
    wide = vectors.astype(F32)
    solved = dot(inv_high[...], vectors) + dot(inv_low[...], vectors) + jnp.concatenate(weights, axis=0) * wide
    norms = jnp.sum(solved * wide, axis=0, keepdims=True)
    near = solved.astype(BF16)
    turned = dot(high_ref[...], near) + dot(low_ref[...], near)
    energy = jnp.sum(turned * solved, axis=0, keepdims=True)
    out_ref[...] = energy / (shots * norms * norms)


def next_powers(where, mine, other, steering, sample, owned, pairs, shots):
    blocks = steering.shape[1]
    order = blocks * TILE
    whole = lambda *shape: pl.BlockSpec(shape, lambda s, m: (0,) * len(shape))
    grid_spec = pltpu.PrefetchScalarGridSpec(
        num_scalar_prefetch=1,
        grid=(1,),
        in_specs=[
            whole(*mine.shape),
            whole(*other.shape),
            own_block(steering.shape, owned),
            whole(2 * order, 2 * order),
            whole(2 * order, 2 * order),
        ],
        out_specs=whole(1, owned),
        scratch_shapes=[
            pltpu.VMEM((order, 2 * order), F32),
            pltpu.VMEM((TILE, PAIR), F32),
            pltpu.VMEM((2 * order, 2 * order), BF16),
            pltpu.VMEM((2 * order, 2 * order), BF16),
        ],
    )
    return pl.pallas_call(
        functools.partial(step_kernel, pairs, shots),
        grid_spec=grid_spec,
        out_shape=jax.ShapeDtypeStruct((1, owned), F32),
        name="step",
        cost_estimate=cost(35),
        compiler_params=pltpu.CompilerParams(vmem_limit_bytes=56 * 1024 * 1024),
    )(where, mine, other, steering, *sample)


def shards(cube, select, phases, jitter):
    snap_count, ang_count = lax.axis_size("snap"), lax.axis_size("ang")
    snap_index, ang_index = lax.axis_index("snap"), lax.axis_index("ang")
    channels = cube.shape[1]
    shots = select.shape[0] * snap_count
    owned = K // (ang_count * snap_count)
    groups = block_groups(channels // TILE)
    pairs = [group_pairs(group) for group in groups]
    slots = [slot for slot, (a, partners) in enumerate(groups[0]) for b in partners]
    core = snap_index % 2
    me = (ang_index * snap_count + snap_index).astype(jnp.int32)
    where = jnp.stack([me, core.astype(jnp.int32)])
    flat = [
        jnp.array([a for a, partners in group] + [b for a, b in group_pairs(group)], jnp.int32) for group in groups
    ]
    table = jnp.concatenate([me[None], jnp.where(core == 0, flat[0], flat[1])])

    steering = all_steering(phases, jitter, max(owned, WIDTH))
    every = [(a, b) for a in range(channels // TILE) for b in range(a + 1)]
    gram, rows = sample_terms(cube, select - snap_index * cube.shape[2], every)
    piece = halve(halve(gram.reshape(-1, TILE), "snap", 0), "snap", 1)
    steering, piece = lax.optimization_barrier((steering, piece))
    energy = local_energy(where, steering, rows, owned)
    powers = scatter_energy(energy) / float(shots * channels * channels)
    for bit in range(2, snap_count.bit_length() - 1):
        piece = halve(piece, "snap", bit)

    def iteration(gathered):
        mine = covariance_half(table, steering, gathered, slots)
        other = swap(mine, "snap", 1)
        return next_powers(where, mine, other, steering, sample, owned, pairs, float(shots))

    gathered = gather_relative(powers)
    gathered, piece = lax.optimization_barrier((gathered, piece))

    others = []
    for m in range(2, snap_count, 2):
        others.append(swap(piece, "snap", m))
    both = jnp.concatenate([piece] + others, axis=0)
    parts = [both, swap(both, "snap", 1)]
    sample = spread(where, parts, every, 2 * channels)
    powers = iteration(gathered)
    return lax.fori_loop(1, ITERS, lambda _, powers: iteration(gather_relative(powers)), powers)[0]


def solution(mesh):
    return jax.shard_map(
        shards,
        mesh=mesh,
        in_specs=(P(None, None, "snap"), P("snap"), P(), P()),
        out_specs=P(("ang", "snap")),
        check_vma=False,
    )
```

```python
import functools
import math

import jax
import jax.numpy as jnp
from jax import lax
from jax.experimental import pallas as pl
from jax.experimental.pallas import tpu as pltpu
from jax.sharding import PartitionSpec as P


RX = 32
GU = 128
GV = 128
Q = 64
ITERS = 3
K = GU * GV

TILE = 128
PAIR = 2 * TILE
WIDTH = 2048
PANEL = 16
AHEAD = 6
F32 = jnp.float32
BF16 = jnp.bfloat16


def nt_dot(left, right):
    return lax.dot_general(left, right, (((1,), (1,)), ((), ())), preferred_element_type=F32)


def dot(left, right):
    return jnp.dot(left, right, preferred_element_type=F32)


def split(x):
    high = x.astype(BF16)
    return high, (x - high.astype(F32)).astype(BF16)


def dot3(left, right):
    left_high, left_low = split(left)
    right_high, right_low = split(right)
    return dot(left_high, right_high) + (dot(left_low, right_high) + dot(left_high, right_low))


def take(x, index):
    return jnp.take_along_axis(x, index, axis=1, mode="promise_in_bounds")


def cost(microseconds):
    return pl.CostEstimate(flops=microseconds * 10**9, bytes_accessed=microseconds * 3 * 10**6, transcendentals=0)


def block_groups(blocks):
    groups = ([], [])
    for a in range(blocks):
        reach = blocks // 2 + (1 if a < blocks // 2 or blocks % 2 else 0)
        groups[a % 2].append((a, [(a + r) % blocks for r in range(reach)]))
    return groups


def group_pairs(group):
    return [(a, b) for a, partners in group for b in partners]


def complex_block(gram):
    real = gram[:TILE, :TILE] + gram[TILE:, TILE:]
    imag = gram[TILE:, :TILE] - gram[:TILE, TILE:]
    return real, imag


def angle_tables(phases, jitter, steps):
    channels = phases.shape[0] * RX
    channel = jnp.arange(channels, dtype=jnp.int32)
    position_x = (channel % RX).astype(F32) + jitter[0]
    position_y = (channel // RX).astype(F32) + jitter[1]
    offsets = jnp.broadcast_to(phases[:, None], (phases.shape[0], RX)).reshape(channels).astype(F32)
    lane = jnp.arange(GV, dtype=jnp.int32)
    row_angle = (2 * steps * lane - GU).astype(F32) / GU
    col_angle = (2 * lane - GV).astype(F32) / GV
    start = math.pi * (position_x[:, None] * row_angle[None, :])
    col = math.pi * (position_y[:, None] * col_angle[None, :]) + 2.0 * math.pi / Q * offsets[:, None]
    turn = jnp.broadcast_to((math.pi * 2.0 / GU) * position_x[:, None], (channels, GV))
    angles = jnp.stack([start, col, turn])
    return jnp.cos(angles), jnp.sin(angles)


def fill_blocks(chunk, first, real_ref, imag_ref, out_ref):
    steps = out_ref.shape[3] // GV
    spot = jnp.full((TILE, GV), chunk, jnp.int32)

    def block(b, _):
        rows = pl.ds(pl.multiple_of((first + b) * TILE, TILE), TILE)
        first_real, first_imag = take(real_ref[0, rows, :], spot), take(imag_ref[0, rows, :], spot)
        across_real, across_imag = real_ref[1, rows, :], imag_ref[1, rows, :]
        real = across_real * first_real - across_imag * first_imag
        imag = across_real * first_imag + across_imag * first_real
        by_real, by_imag = real_ref[2, rows, :], imag_ref[2, rows, :]
        for step in range(steps):
            if step:
                real, imag = real * by_real - imag * by_imag, real * by_imag + imag * by_real
            columns = slice(step * GV, (step + 1) * GV)
            out_ref[0, b, :TILE, columns] = real.astype(BF16)
            out_ref[0, b, TILE:, columns] = imag.astype(BF16)
        return 0

    lax.fori_loop(0, out_ref.shape[1], block, 0, unroll=True)


def near_kernel(chunk_of, where_ref, real_ref, imag_ref, shots_ref, out_ref, energy_ref, beams):
    step = pl.program_id(1)
    count = out_ref.shape[1]
    fill_blocks(chunk_of(pl.program_id(0), where_ref), step * count, real_ref, imag_ref, out_ref)

    @pl.when(step == 0)
    def _():
        beams[...] = jnp.zeros_like(beams)

    beams[...] += dot(shots_ref[...], out_ref[0].reshape(count * PAIR, out_ref.shape[3]))

    @pl.when(step == pl.num_programs(1) - 1)
    def _():
        energy_ref[0] = jnp.sum(beams[...] * beams[...], axis=0, keepdims=True)


def far_kernel(chunk_of, where_ref, real_ref, imag_ref, before_ref, out_ref):
    count = out_ref.shape[1]
    fill_blocks(chunk_of(pl.program_id(0), where_ref), pl.program_id(1) * count, real_ref, imag_ref, out_ref)


def fill_steering(where, tables, blocks, owned, width, mask, shots=None, before=None):
    near = lax.axis_size("snap") * owned // width
    per = width // owned
    count = 2 - blocks % 2

    def chunk_of(step, m):
        return (m[0] // (per * near) ^ mask) * near + step

    in_specs = [pl.BlockSpec(table.shape, lambda s, b, m: (0, 0, 0)) for table in tables]
    out_specs = [pl.BlockSpec((1, count, PAIR, width), lambda s, b, m: (chunk_of(s, m), b, 0, 0))]
    out_shape = [jax.ShapeDtypeStruct((K // width, blocks, PAIR, width), BF16)]
    if before is None:
        kernel, last, aliases = near_kernel, shots, {}
        in_specs.append(pl.BlockSpec((shots.shape[0], count * PAIR), lambda s, b, m: (0, b)))
        out_specs.append(pl.BlockSpec((1, 1, width), lambda s, b, m: (s, 0, 0)))
        out_shape.append(jax.ShapeDtypeStruct((near, 1, width), F32))
        scratch = [pltpu.VMEM((shots.shape[0], width), F32)]
    else:
        kernel, last, aliases, scratch = far_kernel, before, {3: 0}, []
        in_specs.append(pl.BlockSpec(memory_space=pl.ANY))
    return pl.pallas_call(
        functools.partial(kernel, chunk_of),
        grid_spec=pltpu.PrefetchScalarGridSpec(
            num_scalar_prefetch=1,
            grid=(near, blocks // count),
            in_specs=in_specs,
            out_specs=out_specs,
            scratch_shapes=scratch,
        ),
        out_shape=out_shape,
        input_output_aliases=aliases,
        name="near_steering" if before is None else "far_steering",
        cost_estimate=cost(8 if before is None else 5),
    )(where, *tables, last)


def sample_kernel(pairs, cube_ref, select_ref, gram_ref, shots_ref):
    cells = cube_ref.shape[2]
    shots = select_ref.shape[1]
    chosen = lax.broadcasted_iota(jnp.int32, (cells, shots), 0) == select_ref[...]
    chosen = jnp.where(chosen, 1.0, 0.0).astype(BF16)
    blocks = cube_ref.shape[1] // TILE
    picked = []
    for block in range(blocks):
        rows = slice(block * TILE, (block + 1) * TILE)
        both = jnp.concatenate([cube_ref[0, rows, :], cube_ref[1, rows, :]], axis=0)
        found = dot(both, chosen)
        picked.append(found.astype(BF16))
        flat = found.T
        columns = slice(block * PAIR, (block + 1) * PAIR)
        shots_ref[:shots, columns] = flat.astype(BF16)
        shots_ref[shots:, columns] = jnp.concatenate([flat[:, TILE:], -flat[:, :TILE]], axis=1).astype(BF16)
    for index, (a, b) in enumerate(pairs):
        real, imag = complex_block(nt_dot(picked[a], picked[b]))
        gram_ref[2 * index] = real
        gram_ref[2 * index + 1] = imag


def sample_terms(cube, select, pairs):
    shots = select.shape[0]
    return pl.pallas_call(
        functools.partial(sample_kernel, pairs),
        out_shape=[
            jax.ShapeDtypeStruct((2 * len(pairs), TILE, TILE), F32),
            jax.ShapeDtypeStruct((2 * shots, 2 * cube.shape[1]), BF16),
        ],
        name="sample",
        cost_estimate=cost(4),
    )(cube, select[None, :])


def swap(x, axis, mask):
    size = lax.axis_size(axis)
    return lax.ppermute(x, axis, [(i, i ^ mask) for i in range(size)])


def halve(x, axis, bit):
    half = x.shape[0] // 2
    high = (lax.axis_index(axis) >> bit) % 2
    keep = lax.dynamic_slice_in_dim(x, high * half, half, 0)
    give = lax.dynamic_slice_in_dim(x, (1 - high) * half, half, 0)
    return keep + swap(give, axis, 1 << bit)


def piece_start(index, size, rows):
    start = 0
    for bit in range(size.bit_length() - 1):
        rows = rows // 2
        start = start + (index >> bit) % 2 * rows
    return start


def scatter_energy(rows):
    snap, index = lax.axis_size("snap"), lax.axis_index("snap")
    halves = rows.reshape(snap // 2, 2, rows.shape[1])
    core, high = index % 2, index // 2
    mine = lax.dynamic_index_in_dim(halves, core, 1, keepdims=False)
    give = lax.dynamic_index_in_dim(halves, 1 - core, 1, keepdims=False)
    both = mine + swap(give, "snap", 1)
    total = lax.dynamic_slice_in_dim(both, high, 1, 0)
    for m in range(1, snap // 2):
        total = total + swap(lax.dynamic_slice_in_dim(both, high ^ m, 1, 0), "snap", 2 * m)
    return total


def gather_relative(x):
    snap, ang = lax.axis_size("snap"), lax.axis_size("ang")
    x = jnp.concatenate([x, swap(x, "snap", 1)], axis=0)
    parts = [x]
    for m in range(2, snap, 2):
        parts.append(swap(x, "snap", m))
    x = jnp.concatenate(parts, axis=0)
    parts = [x]
    for m in range(1, ang):
        parts.append(swap(x, "ang", m))
    return parts


def covariance_kernel(slots, table_ref, steering_ref, *refs):
    *parts, out_ref, powers_ref, scaled, total = refs
    step = pl.program_id(0)
    owned = powers_ref.shape[1]
    per = steering_ref.shape[3] // owned
    low = table_ref[0] % per

    @pl.when(step == 0)
    def _():
        total[...] = jnp.zeros_like(total)
        for n, part in enumerate(parts):
            powers_ref[n * part.shape[0] : (n + 1) * part.shape[0], :] = part[...]

    weights = jnp.concatenate([powers_ref[pl.ds(step * per + (q ^ low), 1), :] for q in range(per)], axis=1)
    used = max(slots) + 1
    for slot in range(used):
        scaled[slot] = (steering_ref[0, table_ref[1 + slot]].astype(F32) * weights).astype(BF16)
    for n, slot in enumerate(slots):
        total[n] += nt_dot(scaled[slot], steering_ref[0, table_ref[1 + used + n]])

    @pl.when(step == pl.num_programs(0) - 1)
    def _():
        for n in range(len(slots)):
            real, imag = complex_block(total[n])
            out_ref[2 * n] = real
            out_ref[2 * n + 1] = imag


def covariance_half(table, steering, powers, slots):
    chunks, blocks, pair, width = steering.shape
    rows, owned = powers[0].shape
    per = width // owned
    count = len(slots)
    grid_spec = pltpu.PrefetchScalarGridSpec(
        num_scalar_prefetch=1,
        grid=(chunks,),
        in_specs=[
            pl.BlockSpec((1, blocks, pair, width), lambda s, t: (s ^ (t[0] // per), 0, 0, 0)),
        ]
        + [pl.BlockSpec((rows, owned), lambda s, t: (0, 0))] * len(powers),
        out_specs=pl.BlockSpec((2 * count, TILE, TILE), lambda s, t: (0, 0, 0)),
        scratch_shapes=[
            pltpu.VMEM((rows * len(powers), owned), F32),
            pltpu.VMEM((max(slots) + 1, PAIR, width), BF16),
            pltpu.VMEM((count, PAIR, PAIR), F32),
        ],
    )
    return pl.pallas_call(
        functools.partial(covariance_kernel, slots),
        grid_spec=grid_spec,
        out_shape=jax.ShapeDtypeStruct((2 * count, TILE, TILE), F32),
        name="covariance",
        cost_estimate=cost(17),
    )(table, steering, *powers)


def embed(store, i, j, real, imag):
    top, left = i * PAIR, j * PAIR
    store(slice(top, top + TILE), slice(left, left + TILE), real)
    store(slice(top, top + TILE), slice(left + TILE, left + PAIR), -imag)
    store(slice(top + TILE, top + PAIR), slice(left, left + TILE), imag)
    store(slice(top + TILE, top + PAIR), slice(left + TILE, left + PAIR), real)


def spread_kernel(pairs, size, where_ref, *refs):
    *parts, high_ref, low_ref, whole = refs
    half = size // 2
    piece = parts[0].shape[0] // half
    for core, part in enumerate(parts):
        for n in range(half):
            start = piece_start((where_ref[0] % size) ^ (2 * n + core), size, whole.shape[0])
            whole[pl.ds(pl.multiple_of(start, 8), piece), :] = part[n * piece : (n + 1) * piece, :]

    def store(rows, columns, value):
        high, low = split(value)
        high_ref[rows, columns] = high
        low_ref[rows, columns] = low

    for index, (a, b) in enumerate(pairs):
        real = whole[2 * index * TILE : (2 * index + 1) * TILE, :]
        imag = whole[(2 * index + 1) * TILE : (2 * index + 2) * TILE, :]
        embed(store, a, b, real, imag)
        if a != b:
            embed(store, b, a, real.T, -imag.T)


def spread(where, parts, pairs, order):
    size = lax.axis_size("snap")
    whole = lambda shape: pl.BlockSpec(shape, lambda s, m: (0, 0))
    return pl.pallas_call(
        functools.partial(spread_kernel, pairs, size),
        grid_spec=pltpu.PrefetchScalarGridSpec(
            num_scalar_prefetch=1,
            grid=(1,),
            in_specs=[whole(part.shape) for part in parts],
            out_specs=[whole((order, order))] * 2,
            scratch_shapes=[pltpu.VMEM((2 * len(pairs) * TILE, TILE), F32)],
        ),
        out_shape=[jax.ShapeDtypeStruct((order, order), BF16)] * 2,
        name="spread",
        cost_estimate=cost(3),
    )(where, *parts)


def invert_tile(tile):
    lane_all = lax.broadcasted_iota(jnp.int32, (TILE, TILE), 1)
    lane = lax.broadcasted_iota(jnp.int32, (PANEL, TILE), 1)
    sublane = lax.broadcasted_iota(jnp.int32, (PANEL, TILE), 0)

    def panel(step, _):
        base = pl.multiple_of(step * PANEL, PANEL)
        row_real, row_imag = tile[pl.ds(base, PANEL), :TILE], tile[pl.ds(base, PANEL), TILE:]

        def spread_column(j):
            spot = jnp.full((PANEL, TILE), base + j, jnp.int32)
            return take(row_real, spot), take(row_imag, spot)

        columns = {j: spread_column(j) for j in range(AHEAD)}
        real, imag = tile[:, :TILE], tile[:, TILE:]
        pattern = base + lane_all % PANEL
        sides = jnp.where((lane_all // PANEL) % 2 == 0, take(real, pattern), take(imag, pattern))
        high = sides.astype(BF16).astype(F32)
        left = jnp.where(lane_all // (2 * PANEL) == 1, sides - high, high).astype(BF16)
        for p in range(PANEL):
            if p + AHEAD < PANEL:
                columns[p + AHEAD] = spread_column(p + AHEAD)
            here = sublane == p
            hit = lane == base + p
            own_real, own_imag = columns.pop(p)
            inverse = 1.0 / own_real[p : p + 1, :]
            own_real = jnp.where(here, 1.0 - inverse, own_real * inverse)
            own_imag = jnp.where(here, 0.0, own_imag * inverse)

            def reduce(real, imag):
                pivot_real, pivot_imag = real[p : p + 1, :], imag[p : p + 1, :]
                return (
                    real - (own_real * pivot_real - own_imag * pivot_imag),
                    imag - (own_real * pivot_imag + own_imag * pivot_real),
                )

            row_real = jnp.where(hit, jnp.where(here, 1.0, 0.0), row_real)
            row_imag = jnp.where(hit, 0.0, row_imag)
            row_real, row_imag = reduce(row_real, row_imag)
            for j in columns:
                columns[j] = reduce(*columns[j])
        rows = jnp.concatenate([row_real, row_imag], axis=1)
        high, low = split(rows)
        turned_high = jnp.concatenate([-high[:, TILE:], high[:, :TILE]], axis=1)
        turned_low = jnp.concatenate([-low[:, TILE:], low[:, :TILE]], axis=1)
        right = [high, turned_high, high, turned_high, low, turned_low]
        right += [jnp.zeros_like(low)] * (TILE // PANEL - len(right))
        update = dot(left, jnp.concatenate(right, axis=0))
        inside = lane_all // PANEL == step
        tile[:, :TILE] = jnp.where(inside, 0.0, real) - update[:, :TILE]
        tile[:, TILE:] = jnp.where(inside, 0.0, imag) - update[:, TILE:]
        tile[pl.ds(base, PANEL), :] = rows
        return 0

    lax.fori_loop(0, TILE // PANEL, panel, 0)


def step_kernel(
    pairs, shots, where_ref, mine_any, other_any, steering_any, high_any, low_any, out_ref,
    mine_ref, other_ref, steering_ref, high_ref, low_ref, matrix, tile, inv_high, inv_low, copied
):
    order = matrix.shape[0]
    blocks = order // TILE
    owned = steering_ref.shape[2]
    per = steering_any.shape[3] // owned
    column = pl.multiple_of((where_ref[0] % per) * owned, owned)
    own_steering = steering_any.at[where_ref[0] // per, :, :, pl.ds(column, owned)]
    sources = [mine_any, other_any, own_steering, high_any, low_any]
    targets = [mine_ref, other_ref, steering_ref, high_ref, low_ref]
    copies = [pltpu.make_async_copy(a, b, copied.at[n]) for n, (a, b) in enumerate(zip(sources, targets))]
    for copy in copies:
        copy.start()
    for copy in copies[:2]:
        copy.wait()

    def rows(i):
        return slice(i * TILE, (i + 1) * TILE)

    def cols(i, part):
        return slice(part * order + i * TILE, part * order + (i + 1) * TILE)

    def put(group, ref):
        for index, (a, b) in enumerate(pairs[group]):
            real, imag = ref[2 * index], ref[2 * index + 1]
            if a == b:
                matrix[rows(a), cols(a, 0)] = 0.5 * (real + real.T)
                matrix[rows(a), cols(a, 1)] = 0.5 * (imag - imag.T)
            else:
                matrix[rows(a), cols(b, 0)] = real
                matrix[rows(a), cols(b, 1)] = imag
                matrix[rows(b), cols(a, 0)] = real.T
                matrix[rows(b), cols(a, 1)] = -imag.T

    @pl.when(where_ref[1] == 0)
    def _():
        put(0, mine_ref)
        put(1, other_ref)

    @pl.when(where_ref[1] != 0)
    def _():
        put(1, mine_ref)
        put(0, other_ref)

    diagonal = lax.broadcasted_iota(jnp.int32, (TILE, TILE), 0) == lax.broadcasted_iota(jnp.int32, (TILE, TILE), 1)
    trace = jnp.zeros((1, 1), F32)
    for i in range(blocks):
        kept = jnp.where(diagonal, matrix[rows(i), cols(i, 0)], 0.0)
        trace = trace + jnp.sum(jnp.sum(kept, axis=0, keepdims=True), axis=1, keepdims=True)
    matrix[...] = matrix[...] * (1.0 / trace)
    for i in range(blocks):
        matrix[rows(i), cols(i, 0)] += jnp.where(diagonal, 1.0 / order, 0.0)

    unit = jnp.where(diagonal, 1.0, 0.0)
    nothing = jnp.zeros((TILE, TILE), F32)
    for k in range(blocks):
        tile[:, :TILE] = matrix[rows(k), cols(k, 0)]
        tile[:, TILE:] = matrix[rows(k), cols(k, 1)]
        invert_tile(tile)
        column = jnp.concatenate([matrix[:, cols(k, 0)], matrix[:, cols(k, 1)]], axis=1)
        matrix[rows(k), cols(k, 0)] = unit
        matrix[rows(k), cols(k, 1)] = nothing
        row_real, row_imag = matrix[rows(k), :order], matrix[rows(k), order:]
        panel = jnp.concatenate([row_real, row_imag], axis=1)
        turned = jnp.concatenate([-row_imag, row_real], axis=1)
        row = dot3(tile[...], jnp.concatenate([panel, turned], axis=0))
        row_turned = jnp.concatenate([-row[:, order:], row[:, :order]], axis=1)
        tall = jnp.concatenate([row, row_turned], axis=0)
        for i in range(blocks):
            if i == k:
                matrix[rows(k), :] = row
            else:
                matrix[rows(i), cols(k, 0)] = nothing
                matrix[rows(i), cols(k, 1)] = nothing
                matrix[rows(i), :] -= dot3(column[rows(i)], tall)

    def store(at_rows, at_columns, value):
        high, low = split(value)
        inv_high[at_rows, at_columns] = high
        inv_low[at_rows, at_columns] = low

    weights = []
    for i in range(blocks):
        for j in range(blocks):
            real, imag = matrix[rows(i), cols(j, 0)], matrix[rows(i), cols(j, 1)]
            if i == j:
                weight = jnp.sum(jnp.where(diagonal, real, 0.0), axis=1, keepdims=True)
                weights += [weight, weight]
                real = jnp.where(diagonal, 0.0, real)
            embed(store, i, j, real, imag)
    for copy in copies[2:]:
        copy.wait()
    vectors = steering_ref[...].reshape(2 * order, owned)
    wide = vectors.astype(F32)
    solved = dot(inv_high[...], vectors) + dot(inv_low[...], vectors) + jnp.concatenate(weights, axis=0) * wide
    norms = jnp.sum(solved * wide, axis=0, keepdims=True)
    near = solved.astype(BF16)
    turned = dot(high_ref[...], near) + dot(low_ref[...], near)
    energy = jnp.sum(turned * solved, axis=0, keepdims=True)
    out_ref[...] = energy / (shots * norms * norms)


def next_powers(where, mine, other, steering, sample, owned, pairs, shots):
    blocks = steering.shape[1]
    order = blocks * TILE
    square = pltpu.VMEM((2 * order, 2 * order), BF16)
    operands = (mine, other, steering, *sample)
    grid_spec = pltpu.PrefetchScalarGridSpec(
        num_scalar_prefetch=1,
        grid=(1,),
        in_specs=[pl.BlockSpec(memory_space=pl.ANY)] * len(operands),
        out_specs=pl.BlockSpec((1, owned), lambda s, m: (0, 0)),
        scratch_shapes=[
            pltpu.VMEM(mine.shape, F32),
            pltpu.VMEM(other.shape, F32),
            pltpu.VMEM((blocks, PAIR, owned), BF16),
            square,
            square,
            pltpu.VMEM((order, 2 * order), F32),
            pltpu.VMEM((TILE, PAIR), F32),
            square,
            square,
            pltpu.SemaphoreType.DMA((len(operands),)),
        ],
    )
    return pl.pallas_call(
        functools.partial(step_kernel, pairs, shots),
        grid_spec=grid_spec,
        out_shape=jax.ShapeDtypeStruct((1, owned), F32),
        name="step",
        cost_estimate=cost(28),
        compiler_params=pltpu.CompilerParams(vmem_limit_bytes=56 * 1024 * 1024),
    )(where, *operands)


def shards(cube, select, phases, jitter):
    snap_count, ang_count = lax.axis_size("snap"), lax.axis_size("ang")
    snap_index, ang_index = lax.axis_index("snap"), lax.axis_index("ang")
    channels = cube.shape[1]
    shots = select.shape[0] * snap_count
    owned = K // (ang_count * snap_count)
    groups = block_groups(channels // TILE)
    pairs = [group_pairs(group) for group in groups]
    slots = [slot for slot, (a, partners) in enumerate(groups[0]) for b in partners]
    core = snap_index % 2
    me = (ang_index * snap_count + snap_index).astype(jnp.int32)
    where = jnp.stack([me, core.astype(jnp.int32)])
    flat = [
        jnp.array([a for a, partners in group] + [b for a, b in group_pairs(group)], jnp.int32) for group in groups
    ]
    table = jnp.concatenate([me[None], jnp.where(core == 0, flat[0], flat[1])])

    width = max(owned, WIDTH)
    tables = angle_tables(phases, jitter, width // GV)
    every = [(a, b) for a in range(channels // TILE) for b in range(a + 1)]
    gram, rows = sample_terms(cube, select - snap_index * cube.shape[2], every)
    piece = halve(gram.reshape(-1, TILE), "snap", 0)
    for bit in range(1, snap_count.bit_length() - 1):
        piece = halve(piece, "snap", bit)
    steering, energy = fill_steering(where, tables, channels // TILE, owned, width, 0, shots=rows)
    powers = scatter_energy(energy.reshape(snap_count, owned)) / float(shots * channels * channels)
    for mask in range(1, ang_count):
        (steering,) = fill_steering(
            where, tables, channels // TILE, owned, width, mask, before=steering
        )
    gathered = gather_relative(powers)

    def iteration(gathered):
        mine = covariance_half(table, steering, gathered, slots)
        other = swap(mine, "snap", 1)
        return next_powers(where, mine, other, steering, sample, owned, pairs, float(shots))

    gathered, piece = lax.optimization_barrier((gathered, piece))
    others = []
    for m in range(2, snap_count, 2):
        others.append(swap(piece, "snap", m))
    both = jnp.concatenate([piece] + others, axis=0)
    sample = spread(where, [both, swap(both, "snap", 1)], every, 2 * channels)
    powers = iteration(gathered)
    return lax.fori_loop(1, ITERS, lambda _, powers: iteration(gather_relative(powers)), powers)[0]


def solution(mesh):
    return jax.shard_map(
        shards,
        mesh=mesh,
        in_specs=(P(None, None, "snap"), P("snap"), P(), P()),
        out_specs=P(("ang", "snap")),
        check_vma=False,
    )
```

```python
import functools
import math

import jax
import jax.numpy as jnp
from jax import lax
from jax.experimental import pallas as pl
from jax.experimental.pallas import tpu as pltpu
from jax.sharding import PartitionSpec as P


RX = 32
GU = 128
GV = 128
Q = 64
ITERS = 3
K = GU * GV

TILE = 128
PAIR = 2 * TILE
WIDTH = 2048
PANEL = 16
AHEAD = 6
F32 = jnp.float32
BF16 = jnp.bfloat16


def nt_dot(left, right):
    return lax.dot_general(left, right, (((1,), (1,)), ((), ())), preferred_element_type=F32)


def dot(left, right):
    return jnp.dot(left, right, preferred_element_type=F32)


def split(x):
    high = x.astype(BF16)
    return high, (x - high.astype(F32)).astype(BF16)


def dot3(left, right):
    left_high, left_low = split(left)
    right_high, right_low = split(right)
    return dot(left_high, right_high) + (dot(left_low, right_high) + dot(left_high, right_low))


def take(x, index):
    return jnp.take_along_axis(x, index, axis=1, mode="promise_in_bounds")


def cost(microseconds):
    return pl.CostEstimate(flops=microseconds * 10**9, bytes_accessed=microseconds * 3 * 10**6, transcendentals=0)


def block_groups(blocks):
    groups = ([], [])
    for a in range(blocks):
        reach = blocks // 2 + (1 if a < blocks // 2 or blocks % 2 else 0)
        groups[a % 2].append((a, [(a + r) % blocks for r in range(reach)]))
    return groups


def group_pairs(group):
    return [(a, b) for a, partners in group for b in partners]


def complex_block(gram):
    real = gram[:TILE, :TILE] + gram[TILE:, TILE:]
    imag = gram[TILE:, :TILE] - gram[:TILE, TILE:]
    return real, imag


def angle_tables(phases, jitter, steps):
    channels = phases.shape[0] * RX
    channel = jnp.arange(channels, dtype=jnp.int32)
    position_x = (channel % RX).astype(F32) + jitter[0]
    position_y = (channel // RX).astype(F32) + jitter[1]
    offsets = jnp.broadcast_to(phases[:, None], (phases.shape[0], RX)).reshape(channels).astype(F32)
    lane = jnp.arange(GV, dtype=jnp.int32)
    row_angle = jnp.where(lane == GV - 1, 2.0, (2 * steps * lane - GU).astype(F32)) / GU
    col_angle = (2 * lane - GV).astype(F32) / GV
    row = math.pi * (position_x[:, None] * row_angle[None, :])
    col = math.pi * (position_y[:, None] * col_angle[None, :]) + 2.0 * math.pi / Q * offsets[:, None]
    angles = jnp.stack([row, col])
    return jnp.cos(angles), jnp.sin(angles)


def fill_blocks(chunk, first, real_ref, imag_ref, out_ref):
    steps = out_ref.shape[3] // GV
    spot = jnp.full((TILE, GV), chunk, jnp.int32)
    turn = jnp.full((TILE, GV), GV - 1, jnp.int32)

    def block(b, _):
        rows = pl.ds(pl.multiple_of((first + b) * TILE, TILE), TILE)
        first_real, first_imag = take(real_ref[0, rows, :], spot), take(imag_ref[0, rows, :], spot)
        across_real, across_imag = real_ref[1, rows, :], imag_ref[1, rows, :]
        real = across_real * first_real - across_imag * first_imag
        imag = across_real * first_imag + across_imag * first_real
        by_real, by_imag = take(real_ref[0, rows, :], turn), take(imag_ref[0, rows, :], turn)
        for step in range(steps):
            if step:
                real, imag = real * by_real - imag * by_imag, real * by_imag + imag * by_real
            columns = slice(step * GV, (step + 1) * GV)
            out_ref[0, b, :TILE, columns] = real.astype(BF16)
            out_ref[0, b, TILE:, columns] = imag.astype(BF16)
        return 0

    lax.fori_loop(0, out_ref.shape[1], block, 0, unroll=True)


def near_kernel(chunk_of, where_ref, real_ref, imag_ref, shots_ref, out_ref, energy_ref, beams):
    step = pl.program_id(1)
    count = out_ref.shape[1]
    fill_blocks(chunk_of(pl.program_id(0), where_ref), step * count, real_ref, imag_ref, out_ref)

    @pl.when(step == 0)
    def _():
        beams[...] = jnp.zeros_like(beams)

    beams[...] += dot(shots_ref[...], out_ref[0].reshape(count * PAIR, out_ref.shape[3]))

    @pl.when(step == pl.num_programs(1) - 1)
    def _():
        energy_ref[0] = jnp.sum(beams[...] * beams[...], axis=0, keepdims=True)


def far_kernel(chunk_of, where_ref, real_ref, imag_ref, before_ref, out_ref):
    count = out_ref.shape[1]
    fill_blocks(chunk_of(pl.program_id(0), where_ref), pl.program_id(1) * count, real_ref, imag_ref, out_ref)


def fill_steering(where, tables, blocks, owned, width, mask, shots=None, before=None):
    near = lax.axis_size("snap") * owned // width
    per = width // owned
    count = 2 - blocks % 2

    def chunk_of(step, m):
        return (m[0] // (per * near) ^ mask) * near + step

    in_specs = [pl.BlockSpec(table.shape, lambda s, b, m: (0, 0, 0)) for table in tables]
    out_specs = [pl.BlockSpec((1, count, PAIR, width), lambda s, b, m: (chunk_of(s, m), b, 0, 0))]
    out_shape = [jax.ShapeDtypeStruct((K // width, blocks, PAIR, width), BF16)]
    if before is None:
        kernel, last, aliases = near_kernel, shots, {}
        in_specs.append(pl.BlockSpec((shots.shape[0], count * PAIR), lambda s, b, m: (0, b)))
        out_specs.append(pl.BlockSpec((1, 1, width), lambda s, b, m: (s, 0, 0)))
        out_shape.append(jax.ShapeDtypeStruct((near, 1, width), F32))
        scratch = [pltpu.VMEM((shots.shape[0], width), F32)]
    else:
        kernel, last, aliases, scratch = far_kernel, before, {3: 0}, []
        in_specs.append(pl.BlockSpec(memory_space=pl.ANY))
    return pl.pallas_call(
        functools.partial(kernel, chunk_of),
        grid_spec=pltpu.PrefetchScalarGridSpec(
            num_scalar_prefetch=1,
            grid=(near, blocks // count),
            in_specs=in_specs,
            out_specs=out_specs,
            scratch_shapes=scratch,
        ),
        out_shape=out_shape,
        input_output_aliases=aliases,
        name="near_steering" if before is None else "far_steering",
        cost_estimate=cost(8 if before is None else 5),
    )(where, *tables, last)


def sample_kernel(pairs, where_ref, cube_ref, select_ref, keep_ref, give_ref, shots_ref, gram_ref):
    cells = cube_ref.shape[2]
    shots = select_ref.shape[1]
    chosen = lax.broadcasted_iota(jnp.int32, (cells, shots), 0) == select_ref[...]
    chosen = jnp.where(chosen, 1.0, 0.0).astype(BF16)
    blocks = cube_ref.shape[1] // TILE
    picked = []
    for block in range(blocks):
        rows = slice(block * TILE, (block + 1) * TILE)
        both = jnp.concatenate([cube_ref[0, rows, :], cube_ref[1, rows, :]], axis=0)
        found = dot(both, chosen)
        picked.append(found.astype(BF16))
        flat = found.T
        columns = slice(block * PAIR, (block + 1) * PAIR)
        shots_ref[:shots, columns] = flat.astype(BF16)
        shots_ref[shots:, columns] = jnp.concatenate([flat[:, TILE:], -flat[:, :TILE]], axis=1).astype(BF16)
    for index, (a, b) in enumerate(pairs):
        real, imag = complex_block(nt_dot(picked[a], picked[b]))
        gram_ref[2 * index] = real
        gram_ref[2 * index + 1] = imag
    keep_ref[...] = gram_ref[pl.ds(where_ref[1] * len(pairs), len(pairs))]
    give_ref[...] = gram_ref[pl.ds((1 - where_ref[1]) * len(pairs), len(pairs))]


def sample_terms(where, cube, select, pairs):
    shots = select.shape[0]
    whole = lambda *shape: pl.BlockSpec(shape, lambda s, m: (0,) * len(shape))
    half = (len(pairs), TILE, TILE)
    turned = (2 * shots, 2 * cube.shape[1])
    return pl.pallas_call(
        functools.partial(sample_kernel, pairs),
        grid_spec=pltpu.PrefetchScalarGridSpec(
            num_scalar_prefetch=1,
            grid=(1,),
            in_specs=[whole(*cube.shape), whole(1, shots)],
            out_specs=[whole(*half), whole(*half), whole(*turned)],
            scratch_shapes=[pltpu.VMEM((2 * len(pairs), TILE, TILE), F32)],
        ),
        out_shape=[
            jax.ShapeDtypeStruct(half, F32),
            jax.ShapeDtypeStruct(half, F32),
            jax.ShapeDtypeStruct(turned, BF16),
        ],
        name="sample",
        cost_estimate=cost(4),
    )(where, cube, select[None, :])


def swap(x, axis, mask):
    size = lax.axis_size(axis)
    return lax.ppermute(x, axis, [(i, i ^ mask) for i in range(size)])


def halve(x, axis, bit):
    half = x.shape[0] // 2
    high = (lax.axis_index(axis) >> bit) % 2
    keep = lax.dynamic_slice_in_dim(x, high * half, half, 0)
    give = lax.dynamic_slice_in_dim(x, (1 - high) * half, half, 0)
    return keep + swap(give, axis, 1 << bit)


def piece_start(index, size, rows):
    start = 0
    for bit in range(size.bit_length() - 1):
        rows = rows // 2
        start = start + (index >> bit) % 2 * rows
    return start


def scatter_energy(rows):
    snap, index = lax.axis_size("snap"), lax.axis_index("snap")
    halves = rows.reshape(snap // 2, 2, rows.shape[1])
    core, high = index % 2, index // 2
    mine = lax.dynamic_index_in_dim(halves, core, 1, keepdims=False)
    give = lax.dynamic_index_in_dim(halves, 1 - core, 1, keepdims=False)
    both = mine + swap(give, "snap", 1)
    total = lax.dynamic_slice_in_dim(both, high, 1, 0)
    for m in range(1, snap // 2):
        total = total + swap(lax.dynamic_slice_in_dim(both, high ^ m, 1, 0), "snap", 2 * m)
    return total


def gather_relative(x):
    snap, ang = lax.axis_size("snap"), lax.axis_size("ang")
    x = jnp.concatenate([x, swap(x, "snap", 1)], axis=0)
    parts = [x]
    for m in range(2, snap, 2):
        parts.append(swap(x, "snap", m))
    x = jnp.concatenate(parts, axis=0)
    parts = [x]
    for m in range(1, ang):
        parts.append(swap(x, "ang", m))
    return parts


def covariance_kernel(slots, table_ref, steering_ref, *refs):
    *parts, out_ref, powers_ref, scaled, total = refs
    step = pl.program_id(0)
    owned = powers_ref.shape[1]
    per = steering_ref.shape[3] // owned
    low = table_ref[0] % per

    @pl.when(step == 0)
    def _():
        total[...] = jnp.zeros_like(total)
        for n, part in enumerate(parts):
            powers_ref[n * part.shape[0] : (n + 1) * part.shape[0], :] = part[...]

    weights = jnp.concatenate([powers_ref[pl.ds(step * per + (q ^ low), 1), :] for q in range(per)], axis=1)
    used = max(slots) + 1
    for slot in range(used):
        scaled[slot] = (steering_ref[0, table_ref[1 + slot]].astype(F32) * weights).astype(BF16)
    for n, slot in enumerate(slots):
        total[n] += nt_dot(scaled[slot], steering_ref[0, table_ref[1 + used + n]])

    @pl.when(step == pl.num_programs(0) - 1)
    def _():
        for n in range(len(slots)):
            real, imag = complex_block(total[n])
            out_ref[2 * n] = real
            out_ref[2 * n + 1] = imag


def covariance_half(table, steering, powers, slots):
    chunks, blocks, pair, width = steering.shape
    rows, owned = powers[0].shape
    per = width // owned
    count = len(slots)
    grid_spec = pltpu.PrefetchScalarGridSpec(
        num_scalar_prefetch=1,
        grid=(chunks,),
        in_specs=[
            pl.BlockSpec((1, blocks, pair, width), lambda s, t: (s ^ (t[0] // per), 0, 0, 0)),
        ]
        + [pl.BlockSpec((rows, owned), lambda s, t: (0, 0))] * len(powers),
        out_specs=pl.BlockSpec((2 * count, TILE, TILE), lambda s, t: (0, 0, 0)),
        scratch_shapes=[
            pltpu.VMEM((rows * len(powers), owned), F32),
            pltpu.VMEM((max(slots) + 1, PAIR, width), BF16),
            pltpu.VMEM((count, PAIR, PAIR), F32),
        ],
    )
    return pl.pallas_call(
        functools.partial(covariance_kernel, slots),
        grid_spec=grid_spec,
        out_shape=jax.ShapeDtypeStruct((2 * count, TILE, TILE), F32),
        name="covariance",
        cost_estimate=cost(17),
    )(table, steering, *powers)


def spread_kernel(pairs, size, where_ref, *refs):
    *parts, high_ref, low_ref, whole = refs
    half = size // 2
    piece = parts[0].shape[0] // half
    for core, part in enumerate(parts):
        for n in range(half):
            start = piece_start((where_ref[0] % size) ^ (2 * n + core), size, whole.shape[0])
            whole[pl.ds(pl.multiple_of(start, 8), piece), :] = part[n * piece : (n + 1) * piece, :]

    order = high_ref.shape[0]

    def store(i, j, real, imag):
        for part, value in enumerate((real, imag)):
            rows = slice(i * TILE, (i + 1) * TILE)
            columns = slice(part * order + j * TILE, part * order + (j + 1) * TILE)
            high, low = split(value)
            high_ref[rows, columns] = high
            low_ref[rows, columns] = low

    for index, (a, b) in enumerate(pairs):
        real = whole[2 * index * TILE : (2 * index + 1) * TILE, :]
        imag = whole[(2 * index + 1) * TILE : (2 * index + 2) * TILE, :]
        store(a, b, real, imag)
        if a != b:
            store(b, a, real.T, -imag.T)


def spread(where, parts, pairs, order):
    size = lax.axis_size("snap")
    whole = lambda shape: pl.BlockSpec(shape, lambda s, m: (0, 0))
    return pl.pallas_call(
        functools.partial(spread_kernel, pairs, size),
        grid_spec=pltpu.PrefetchScalarGridSpec(
            num_scalar_prefetch=1,
            grid=(1,),
            in_specs=[whole(part.shape) for part in parts],
            out_specs=[whole((order, 2 * order))] * 2,
            scratch_shapes=[pltpu.VMEM((2 * len(pairs) * TILE, TILE), F32)],
        ),
        out_shape=[jax.ShapeDtypeStruct((order, 2 * order), BF16)] * 2,
        name="spread",
        cost_estimate=cost(3),
    )(where, *parts)


def invert_tile(tile):
    lane_all = lax.broadcasted_iota(jnp.int32, (TILE, TILE), 1)
    lane = lax.broadcasted_iota(jnp.int32, (PANEL, TILE), 1)
    sublane = lax.broadcasted_iota(jnp.int32, (PANEL, TILE), 0)

    def panel(step, _):
        base = pl.multiple_of(step * PANEL, PANEL)
        row_real, row_imag = tile[pl.ds(base, PANEL), :TILE], tile[pl.ds(base, PANEL), TILE:]

        def spread_column(j):
            spot = jnp.full((PANEL, TILE), base + j, jnp.int32)
            return take(row_real, spot), take(row_imag, spot)

        columns = {j: spread_column(j) for j in range(AHEAD)}
        real, imag = tile[:, :TILE], tile[:, TILE:]
        pattern = base + lane_all % PANEL
        sides = jnp.where((lane_all // PANEL) % 2 == 0, take(real, pattern), take(imag, pattern))
        high = sides.astype(BF16).astype(F32)
        left = jnp.where(lane_all // (2 * PANEL) == 1, sides - high, high).astype(BF16)
        for p in range(PANEL):
            if p + AHEAD < PANEL:
                columns[p + AHEAD] = spread_column(p + AHEAD)
            here = sublane == p
            hit = lane == base + p
            own_real, own_imag = columns.pop(p)
            inverse = 1.0 / own_real[p : p + 1, :]
            own_real = jnp.where(here, 1.0 - inverse, own_real * inverse)
            own_imag = jnp.where(here, 0.0, own_imag * inverse)

            def reduce(real, imag):
                pivot_real, pivot_imag = real[p : p + 1, :], imag[p : p + 1, :]
                return (
                    real - (own_real * pivot_real - own_imag * pivot_imag),
                    imag - (own_real * pivot_imag + own_imag * pivot_real),
                )

            row_real = jnp.where(hit, jnp.where(here, 1.0, 0.0), row_real)
            row_imag = jnp.where(hit, 0.0, row_imag)
            row_real, row_imag = reduce(row_real, row_imag)
            for j in columns:
                columns[j] = reduce(*columns[j])
        rows = jnp.concatenate([row_real, row_imag], axis=1)
        high, low = split(rows)
        turned_high = jnp.concatenate([-high[:, TILE:], high[:, :TILE]], axis=1)
        turned_low = jnp.concatenate([-low[:, TILE:], low[:, :TILE]], axis=1)
        right = [high, turned_high, high, turned_high, low, turned_low]
        right += [jnp.zeros_like(low)] * (TILE // PANEL - len(right))
        update = dot(left, jnp.concatenate(right, axis=0))
        inside = lane_all // PANEL == step
        tile[:, :TILE] = jnp.where(inside, 0.0, real) - update[:, :TILE]
        tile[:, TILE:] = jnp.where(inside, 0.0, imag) - update[:, TILE:]
        tile[pl.ds(base, PANEL), :] = rows
        return 0

    lax.fori_loop(0, TILE // PANEL, panel, 0)


def step_kernel(
    pairs, shots, where_ref, mine_any, other_any, steering_any, high_any, low_any, out_ref,
    mine_ref, other_ref, steering_ref, high_ref, low_ref, matrix, tile, inv_high, inv_low, copied
):
    order = matrix.shape[0]
    blocks = order // TILE
    owned = steering_ref.shape[2]
    per = steering_any.shape[3] // owned
    column = pl.multiple_of((where_ref[0] % per) * owned, owned)
    own_steering = steering_any.at[where_ref[0] // per, :, :, pl.ds(column, owned)]
    sources = [mine_any, other_any, own_steering, high_any, low_any]
    targets = [mine_ref, other_ref, steering_ref, high_ref, low_ref]
    copies = [pltpu.make_async_copy(a, b, copied.at[n]) for n, (a, b) in enumerate(zip(sources, targets))]
    for copy in copies:
        copy.start()
    for copy in copies[:2]:
        copy.wait()

    def rows(i):
        return slice(i * TILE, (i + 1) * TILE)

    def cols(i, part):
        return slice(part * order + i * TILE, part * order + (i + 1) * TILE)

    def put(group, ref):
        for index, (a, b) in enumerate(pairs[group]):
            real, imag = ref[2 * index], ref[2 * index + 1]
            if a == b:
                matrix[rows(a), cols(a, 0)] = 0.5 * (real + real.T)
                matrix[rows(a), cols(a, 1)] = 0.5 * (imag - imag.T)
            else:
                matrix[rows(a), cols(b, 0)] = real
                matrix[rows(a), cols(b, 1)] = imag
                matrix[rows(b), cols(a, 0)] = real.T
                matrix[rows(b), cols(a, 1)] = -imag.T

    @pl.when(where_ref[1] == 0)
    def _():
        put(0, mine_ref)
        put(1, other_ref)

    @pl.when(where_ref[1] != 0)
    def _():
        put(1, mine_ref)
        put(0, other_ref)

    diagonal = lax.broadcasted_iota(jnp.int32, (TILE, TILE), 0) == lax.broadcasted_iota(jnp.int32, (TILE, TILE), 1)
    trace = jnp.zeros((1, 1), F32)
    for i in range(blocks):
        kept = jnp.where(diagonal, matrix[rows(i), cols(i, 0)], 0.0)
        trace = trace + jnp.sum(jnp.sum(kept, axis=0, keepdims=True), axis=1, keepdims=True)
    matrix[...] = matrix[...] * (1.0 / trace)
    for i in range(blocks):
        matrix[rows(i), cols(i, 0)] += jnp.where(diagonal, 1.0 / order, 0.0)

    unit = jnp.where(diagonal, 1.0, 0.0)
    nothing = jnp.zeros((TILE, TILE), F32)
    for k in range(blocks):
        tile[:, :TILE] = matrix[rows(k), cols(k, 0)]
        tile[:, TILE:] = matrix[rows(k), cols(k, 1)]
        invert_tile(tile)
        column = jnp.concatenate([matrix[:, cols(k, 0)], matrix[:, cols(k, 1)]], axis=1)
        matrix[rows(k), cols(k, 0)] = unit
        matrix[rows(k), cols(k, 1)] = nothing
        row_real, row_imag = matrix[rows(k), :order], matrix[rows(k), order:]
        panel = jnp.concatenate([row_real, row_imag], axis=1)
        turned = jnp.concatenate([-row_imag, row_real], axis=1)
        row = dot3(tile[...], jnp.concatenate([panel, turned], axis=0))
        row_turned = jnp.concatenate([-row[:, order:], row[:, :order]], axis=1)
        tall = jnp.concatenate([row, row_turned], axis=0)
        for i in range(blocks):
            if i == k:
                matrix[rows(k), :] = row
            else:
                matrix[rows(i), cols(k, 0)] = nothing
                matrix[rows(i), cols(k, 1)] = nothing
                matrix[rows(i), :] -= dot3(column[rows(i)], tall)

    weights = []
    lane = lax.broadcasted_iota(jnp.int32, (TILE, 2 * order), 1)
    sublane = lax.broadcasted_iota(jnp.int32, (TILE, 2 * order), 0)
    for i in range(blocks):
        on_diagonal = lane == sublane + i * TILE
        found = matrix[rows(i), :]
        weights.append(jnp.sum(jnp.where(on_diagonal, found, 0.0), axis=1, keepdims=True))
        inv_high[rows(i), :], inv_low[rows(i), :] = split(jnp.where(on_diagonal, 0.0, found))
    for copy in copies[2:]:
        copy.wait()

    def turn(pair):
        return jnp.concatenate([pair, jnp.concatenate([-pair[:, owned:], pair[:, :owned]], axis=1)], axis=0)

    def over_channels(pair):
        total = jnp.sum(pair, axis=0, keepdims=True)
        return total[:, :owned] + total[:, owned:]

    vectors = jnp.concatenate(
        [jnp.concatenate([steering_ref[b, :TILE, :], steering_ref[b, TILE:, :]], axis=1) for b in range(blocks)], axis=0
    )
    wide = vectors.astype(F32)
    right = turn(vectors)
    solved = dot(inv_high[...], right) + dot(inv_low[...], right) + jnp.concatenate(weights, axis=0) * wide
    norms = over_channels(solved * wide)
    right = turn(solved.astype(BF16))
    turned = dot(high_ref[...], right) + dot(low_ref[...], right)
    out_ref[...] = over_channels(turned * solved) / (shots * norms * norms)


def next_powers(where, mine, other, steering, sample, owned, pairs, shots):
    blocks = steering.shape[1]
    order = blocks * TILE
    half = pltpu.VMEM((order, 2 * order), BF16)
    operands = (mine, other, steering, *sample)
    grid_spec = pltpu.PrefetchScalarGridSpec(
        num_scalar_prefetch=1,
        grid=(1,),
        in_specs=[pl.BlockSpec(memory_space=pl.ANY)] * len(operands),
        out_specs=pl.BlockSpec((1, owned), lambda s, m: (0, 0)),
        scratch_shapes=[
            pltpu.VMEM(mine.shape, F32),
            pltpu.VMEM(other.shape, F32),
            pltpu.VMEM((blocks, PAIR, owned), BF16),
            half,
            half,
            pltpu.VMEM((order, 2 * order), F32),
            pltpu.VMEM((TILE, PAIR), F32),
            half,
            half,
            pltpu.SemaphoreType.DMA((len(operands),)),
        ],
    )
    return pl.pallas_call(
        functools.partial(step_kernel, pairs, shots),
        grid_spec=grid_spec,
        out_shape=jax.ShapeDtypeStruct((1, owned), F32),
        name="step",
        cost_estimate=cost(28),
        compiler_params=pltpu.CompilerParams(vmem_limit_bytes=56 * 1024 * 1024),
    )(where, *operands)


def shards(cube, select, phases, jitter):
    snap_count, ang_count = lax.axis_size("snap"), lax.axis_size("ang")
    snap_index, ang_index = lax.axis_index("snap"), lax.axis_index("ang")
    channels = cube.shape[1]
    shots = select.shape[0] * snap_count
    owned = K // (ang_count * snap_count)
    groups = block_groups(channels // TILE)
    pairs = [group_pairs(group) for group in groups]
    slots = [slot for slot, (a, partners) in enumerate(groups[0]) for b in partners]
    core = snap_index % 2
    me = (ang_index * snap_count + snap_index).astype(jnp.int32)
    where = jnp.stack([me, core.astype(jnp.int32)])
    flat = [
        jnp.array([a for a, partners in group] + [b for a, b in group_pairs(group)], jnp.int32) for group in groups
    ]
    table = jnp.concatenate([me[None], jnp.where(core == 0, flat[0], flat[1])])

    width = max(owned, WIDTH)
    tables = angle_tables(phases, jitter, width // GV)
    every = [(a, b) for a in range(channels // TILE) for b in range(a + 1)]
    keep, give, rows = sample_terms(where, cube, select - snap_index * cube.shape[2], every)
    piece = (keep + swap(give, "snap", 1)).reshape(-1, TILE)
    for bit in range(1, snap_count.bit_length() - 1):
        piece = halve(piece, "snap", bit)
    steering, energy = fill_steering(where, tables, channels // TILE, owned, width, 0, shots=rows)
    powers = scatter_energy(energy.reshape(snap_count, owned)) / float(shots * channels * channels)
    for mask in range(1, ang_count):
        (steering,) = fill_steering(
            where, tables, channels // TILE, owned, width, mask, before=steering
        )
    gathered = gather_relative(powers)

    def iteration(gathered):
        mine = covariance_half(table, steering, gathered, slots)
        other = swap(mine, "snap", 1)
        return next_powers(where, mine, other, steering, sample, owned, pairs, float(shots))

    gathered, piece = lax.optimization_barrier((gathered, piece))
    others = []
    for m in range(2, snap_count, 2):
        others.append(swap(piece, "snap", m))
    both = jnp.concatenate([piece] + others, axis=0)
    sample = spread(where, [both, swap(both, "snap", 1)], every, channels)
    powers = iteration(gathered)
    return lax.fori_loop(1, ITERS, lambda _, powers: iteration(gather_relative(powers)), powers)[0]


def solution(mesh):
    return jax.shard_map(
        shards,
        mesh=mesh,
        in_specs=(P(None, None, "snap"), P("snap"), P(), P()),
        out_specs=P(("ang", "snap")),
        check_vma=False,
    )
```

```python
import functools
import math

import jax
import jax.numpy as jnp
from jax import lax
from jax.experimental import pallas as pl
from jax.experimental.pallas import tpu as pltpu
from jax.sharding import PartitionSpec as P


RX = 32
GU = 128
GV = 128
Q = 64
ITERS = 3
K = GU * GV

TILE = 128
PAIR = 2 * TILE
WIDTH = 2048
PANEL = 16
AHEAD = 6
F32 = jnp.float32
BF16 = jnp.bfloat16


def nt_dot(left, right):
    return lax.dot_general(left, right, (((1,), (1,)), ((), ())), preferred_element_type=F32)


def dot(left, right):
    return jnp.dot(left, right, preferred_element_type=F32)


def split(x):
    high = x.astype(BF16)
    return high, (x - high.astype(F32)).astype(BF16)


def dot3(left, right):
    left_high, left_low = split(left)
    right_high, right_low = split(right)
    return dot(left_high, right_high) + (dot(left_low, right_high) + dot(left_high, right_low))


def take(x, index):
    return jnp.take_along_axis(x, index, axis=1, mode="promise_in_bounds")


def cost(microseconds):
    return pl.CostEstimate(flops=microseconds * 10**9, bytes_accessed=microseconds * 3 * 10**6, transcendentals=0)


def block_groups(blocks):
    groups = ([], [])
    for a in range(blocks):
        reach = blocks // 2 + (1 if a < blocks // 2 or blocks % 2 else 0)
        groups[a % 2].append((a, [(a + r) % blocks for r in range(reach)]))
    return groups


def group_pairs(group):
    return [(a, b) for a, partners in group for b in partners]


def complex_block(gram):
    real = gram[:TILE, :TILE] + gram[TILE:, TILE:]
    imag = gram[TILE:, :TILE] - gram[:TILE, TILE:]
    return real, imag


def angle_tables(phases, jitter, steps):
    channels = phases.shape[0] * RX
    channel = jnp.arange(channels, dtype=jnp.int32)
    position_x = (channel % RX).astype(F32) + jitter[0]
    position_y = (channel // RX).astype(F32) + jitter[1]
    offsets = jnp.broadcast_to(phases[:, None], (phases.shape[0], RX)).reshape(channels).astype(F32)
    lane = jnp.arange(GV, dtype=jnp.int32)
    row_angle = jnp.where(lane == GV - 1, 2.0, (2 * steps * lane - GU).astype(F32)) / GU
    col_angle = (2 * lane - GV).astype(F32) / GV
    row = math.pi * (position_x[:, None] * row_angle[None, :])
    col = math.pi * (position_y[:, None] * col_angle[None, :]) + 2.0 * math.pi / Q * offsets[:, None]
    angles = jnp.stack([row, col])
    return jnp.cos(angles), jnp.sin(angles)


def fill_blocks(chunk, first, real_ref, imag_ref, out_ref):
    steps = out_ref.shape[3] // GV
    spot = jnp.full((TILE, GV), chunk, jnp.int32)
    turn = jnp.full((TILE, GV), GV - 1, jnp.int32)

    def block(b, _):
        rows = pl.ds(pl.multiple_of((first + b) * TILE, TILE), TILE)
        first_real, first_imag = take(real_ref[0, rows, :], spot), take(imag_ref[0, rows, :], spot)
        across_real, across_imag = real_ref[1, rows, :], imag_ref[1, rows, :]
        real = across_real * first_real - across_imag * first_imag
        imag = across_real * first_imag + across_imag * first_real
        by_real, by_imag = take(real_ref[0, rows, :], turn), take(imag_ref[0, rows, :], turn)
        for step in range(steps):
            if step:
                real, imag = real * by_real - imag * by_imag, real * by_imag + imag * by_real
            columns = slice(step * GV, (step + 1) * GV)
            out_ref[0, b, :TILE, columns] = real.astype(BF16)
            out_ref[0, b, TILE:, columns] = imag.astype(BF16)
        return 0

    lax.fori_loop(0, out_ref.shape[1], block, 0, unroll=True)


def near_kernel(chunk_of, where_ref, real_ref, imag_ref, shots_ref, out_ref, energy_ref, beams):
    step = pl.program_id(1)
    count = out_ref.shape[1]
    fill_blocks(chunk_of(pl.program_id(0), where_ref), step * count, real_ref, imag_ref, out_ref)

    @pl.when(step == 0)
    def _():
        beams[...] = jnp.zeros_like(beams)

    beams[...] += dot(shots_ref[...], out_ref[0].reshape(count * PAIR, out_ref.shape[3]))

    @pl.when(step == pl.num_programs(1) - 1)
    def _():
        energy_ref[0] = jnp.sum(beams[...] * beams[...], axis=0, keepdims=True)


def far_kernel(chunk_of, where_ref, real_ref, imag_ref, before_ref, out_ref):
    count = out_ref.shape[1]
    fill_blocks(chunk_of(pl.program_id(0), where_ref), pl.program_id(1) * count, real_ref, imag_ref, out_ref)


def fill_steering(where, tables, blocks, owned, width, mask, shots=None, before=None):
    near = lax.axis_size("snap") * owned // width
    per = width // owned
    count = 2 - blocks % 2

    def chunk_of(step, m):
        return (m[0] // (per * near) ^ mask) * near + step

    in_specs = [pl.BlockSpec(table.shape, lambda s, b, m: (0, 0, 0)) for table in tables]
    out_specs = [pl.BlockSpec((1, count, PAIR, width), lambda s, b, m: (chunk_of(s, m), b, 0, 0))]
    out_shape = [jax.ShapeDtypeStruct((K // width, blocks, PAIR, width), BF16)]
    if before is None:
        kernel, last, aliases = near_kernel, shots, {}
        in_specs.append(pl.BlockSpec((shots.shape[0], count * PAIR), lambda s, b, m: (0, b)))
        out_specs.append(pl.BlockSpec((1, 1, width), lambda s, b, m: (s, 0, 0)))
        out_shape.append(jax.ShapeDtypeStruct((near, 1, width), F32))
        scratch = [pltpu.VMEM((shots.shape[0], width), F32)]
    else:
        kernel, last, aliases, scratch = far_kernel, before, {3: 0}, []
        in_specs.append(pl.BlockSpec(memory_space=pl.ANY))
    return pl.pallas_call(
        functools.partial(kernel, chunk_of),
        grid_spec=pltpu.PrefetchScalarGridSpec(
            num_scalar_prefetch=1,
            grid=(near, blocks // count),
            in_specs=in_specs,
            out_specs=out_specs,
            scratch_shapes=scratch,
        ),
        out_shape=out_shape,
        input_output_aliases=aliases,
        name="near_steering" if before is None else "far_steering",
        cost_estimate=cost(8 if before is None else 5),
    )(where, *tables, last)


def sample_kernel(pairs, where_ref, cube_ref, select_ref, keep_ref, give_ref, shots_ref, gram_ref):
    cells = cube_ref.shape[2]
    shots = select_ref.shape[1]
    chosen = lax.broadcasted_iota(jnp.int32, (cells, shots), 0) == select_ref[...]
    chosen = jnp.where(chosen, 1.0, 0.0).astype(BF16)
    blocks = cube_ref.shape[1] // TILE
    picked = []
    for block in range(blocks):
        rows = slice(block * TILE, (block + 1) * TILE)
        both = jnp.concatenate([cube_ref[0, rows, :], cube_ref[1, rows, :]], axis=0)
        found = dot(both, chosen)
        picked.append(found.astype(BF16))
        flat = found.T
        columns = slice(block * PAIR, (block + 1) * PAIR)
        shots_ref[:shots, columns] = flat.astype(BF16)
        shots_ref[shots:, columns] = jnp.concatenate([flat[:, TILE:], -flat[:, :TILE]], axis=1).astype(BF16)
    for index, (a, b) in enumerate(pairs):
        real, imag = complex_block(nt_dot(picked[a], picked[b]))
        gram_ref[2 * index] = real
        gram_ref[2 * index + 1] = imag
    keep_ref[...] = gram_ref[pl.ds(where_ref[1] * len(pairs), len(pairs))]
    give_ref[...] = gram_ref[pl.ds((1 - where_ref[1]) * len(pairs), len(pairs))]


def sample_terms(where, cube, select, pairs):
    shots = select.shape[0]
    whole = lambda *shape: pl.BlockSpec(shape, lambda s, m: (0,) * len(shape))
    half = (len(pairs), TILE, TILE)
    turned = (2 * shots, 2 * cube.shape[1])
    return pl.pallas_call(
        functools.partial(sample_kernel, pairs),
        grid_spec=pltpu.PrefetchScalarGridSpec(
            num_scalar_prefetch=1,
            grid=(1,),
            in_specs=[whole(*cube.shape), whole(1, shots)],
            out_specs=[whole(*half), whole(*half), whole(*turned)],
            scratch_shapes=[pltpu.VMEM((2 * len(pairs), TILE, TILE), F32)],
        ),
        out_shape=[
            jax.ShapeDtypeStruct(half, F32),
            jax.ShapeDtypeStruct(half, F32),
            jax.ShapeDtypeStruct(turned, BF16),
        ],
        name="sample",
        cost_estimate=cost(4),
    )(where, cube, select[None, :])


def swap(x, axis, mask):
    size = lax.axis_size(axis)
    return lax.ppermute(x, axis, [(i, i ^ mask) for i in range(size)])


def halve(x, axis, bit):
    half = x.shape[0] // 2
    high = (lax.axis_index(axis) >> bit) % 2
    keep = lax.dynamic_slice_in_dim(x, high * half, half, 0)
    give = lax.dynamic_slice_in_dim(x, (1 - high) * half, half, 0)
    return keep + swap(give, axis, 1 << bit)


def piece_start(index, size, rows):
    start = 0
    for bit in range(size.bit_length() - 1):
        rows = rows // 2
        start = start + (index >> bit) % 2 * rows
    return start


def scatter_energy(rows):
    snap, index = lax.axis_size("snap"), lax.axis_index("snap")
    halves = rows.reshape(snap // 2, 2, rows.shape[1])
    core, high = index % 2, index // 2
    mine = lax.dynamic_index_in_dim(halves, core, 1, keepdims=False)
    give = lax.dynamic_index_in_dim(halves, 1 - core, 1, keepdims=False)
    both = mine + swap(give, "snap", 1)
    total = lax.dynamic_slice_in_dim(both, high, 1, 0)
    for m in range(1, snap // 2):
        total = total + swap(lax.dynamic_slice_in_dim(both, high ^ m, 1, 0), "snap", 2 * m)
    return total


def gather_relative(x):
    snap, ang = lax.axis_size("snap"), lax.axis_size("ang")
    x = jnp.concatenate([x, swap(x, "snap", 1)], axis=0)
    parts = [x]
    for m in range(2, snap, 2):
        parts.append(swap(x, "snap", m))
    x = jnp.concatenate(parts, axis=0)
    parts = [x]
    for m in range(1, ang):
        parts.append(swap(x, "ang", m))
    return parts


def covariance_kernel(slots, table_ref, steering_ref, *refs):
    *parts, out_ref, powers_ref, scaled, total = refs
    step = pl.program_id(0)
    owned = powers_ref.shape[1]
    per = steering_ref.shape[3] // owned
    low = table_ref[0] % per

    @pl.when(step == 0)
    def _():
        total[...] = jnp.zeros_like(total)
        for n, part in enumerate(parts):
            powers_ref[n * part.shape[0] : (n + 1) * part.shape[0], :] = part[...]

    weights = jnp.concatenate([powers_ref[pl.ds(step * per + (q ^ low), 1), :] for q in range(per)], axis=1)
    used = max(slots) + 1
    for slot in range(used):
        scaled[slot] = (steering_ref[0, table_ref[1 + slot]].astype(F32) * weights).astype(BF16)
    for n, slot in enumerate(slots):
        total[n] += nt_dot(scaled[slot], steering_ref[0, table_ref[1 + used + n]])

    @pl.when(step == pl.num_programs(0) - 1)
    def _():
        for n in range(len(slots)):
            real, imag = complex_block(total[n])
            out_ref[2 * n] = real
            out_ref[2 * n + 1] = imag


def covariance_half(table, steering, powers, slots):
    chunks, blocks, pair, width = steering.shape
    rows, owned = powers[0].shape
    per = width // owned
    count = len(slots)
    grid_spec = pltpu.PrefetchScalarGridSpec(
        num_scalar_prefetch=1,
        grid=(chunks,),
        in_specs=[
            pl.BlockSpec((1, blocks, pair, width), lambda s, t: (s ^ (t[0] // per), 0, 0, 0)),
        ]
        + [pl.BlockSpec((rows, owned), lambda s, t: (0, 0))] * len(powers),
        out_specs=pl.BlockSpec((2 * count, TILE, TILE), lambda s, t: (0, 0, 0)),
        scratch_shapes=[
            pltpu.VMEM((rows * len(powers), owned), F32),
            pltpu.VMEM((max(slots) + 1, PAIR, width), BF16),
            pltpu.VMEM((count, PAIR, PAIR), F32),
        ],
    )
    return pl.pallas_call(
        functools.partial(covariance_kernel, slots),
        grid_spec=grid_spec,
        out_shape=jax.ShapeDtypeStruct((2 * count, TILE, TILE), F32),
        name="covariance",
        cost_estimate=cost(17),
    )(table, steering, *powers)


def spread_kernel(pairs, size, where_ref, *refs):
    *parts, high_ref, low_ref, whole = refs
    half = size // 2
    piece = parts[0].shape[0] // half
    for core, part in enumerate(parts):
        for n in range(half):
            start = piece_start((where_ref[0] % size) ^ (2 * n + core), size, whole.shape[0])
            whole[pl.ds(pl.multiple_of(start, 8), piece), :] = part[n * piece : (n + 1) * piece, :]

    order = high_ref.shape[0]

    def store(i, j, real, imag):
        for part, value in enumerate((real, imag)):
            rows = slice(i * TILE, (i + 1) * TILE)
            columns = slice(part * order + j * TILE, part * order + (j + 1) * TILE)
            high, low = split(value)
            high_ref[rows, columns] = high
            low_ref[rows, columns] = low

    for index, (a, b) in enumerate(pairs):
        real = whole[2 * index * TILE : (2 * index + 1) * TILE, :]
        imag = whole[(2 * index + 1) * TILE : (2 * index + 2) * TILE, :]
        store(a, b, real, imag)
        if a != b:
            store(b, a, real.T, -imag.T)


def spread(where, parts, pairs, order):
    size = lax.axis_size("snap")
    whole = lambda shape: pl.BlockSpec(shape, lambda s, m: (0, 0))
    return pl.pallas_call(
        functools.partial(spread_kernel, pairs, size),
        grid_spec=pltpu.PrefetchScalarGridSpec(
            num_scalar_prefetch=1,
            grid=(1,),
            in_specs=[whole(part.shape) for part in parts],
            out_specs=[whole((order, 2 * order))] * 2,
            scratch_shapes=[pltpu.VMEM((2 * len(pairs) * TILE, TILE), F32)],
        ),
        out_shape=[jax.ShapeDtypeStruct((order, 2 * order), BF16)] * 2,
        name="spread",
        cost_estimate=cost(3),
    )(where, *parts)


def invert_tile(tile):
    lane_all = lax.broadcasted_iota(jnp.int32, (TILE, TILE), 1)
    lane = lax.broadcasted_iota(jnp.int32, (PANEL, TILE), 1)
    sublane = lax.broadcasted_iota(jnp.int32, (PANEL, TILE), 0)

    def panel(step, _):
        base = pl.multiple_of(step * PANEL, PANEL)
        row_real, row_imag = tile[pl.ds(base, PANEL), :TILE], tile[pl.ds(base, PANEL), TILE:]

        def spread_column(j):
            spot = jnp.full((PANEL, TILE), base + j, jnp.int32)
            return take(row_real, spot), take(row_imag, spot)

        columns = {j: spread_column(j) for j in range(AHEAD)}
        real, imag = tile[:, :TILE], tile[:, TILE:]
        pattern = base + lane_all % PANEL
        sides = jnp.where((lane_all // PANEL) % 2 == 0, take(real, pattern), take(imag, pattern))
        high = sides.astype(BF16).astype(F32)
        left = jnp.where(lane_all // (2 * PANEL) == 1, sides - high, high).astype(BF16)
        for p in range(PANEL):
            if p + AHEAD < PANEL:
                columns[p + AHEAD] = spread_column(p + AHEAD)
            here = sublane == p
            hit = lane == base + p
            own_real, own_imag = columns.pop(p)
            inverse = 1.0 / own_real[p : p + 1, :]
            own_real = jnp.where(here, 1.0 - inverse, own_real * inverse)
            own_imag = jnp.where(here, 0.0, own_imag * inverse)

            def reduce(real, imag):
                pivot_real, pivot_imag = real[p : p + 1, :], imag[p : p + 1, :]
                return (
                    real - (own_real * pivot_real - own_imag * pivot_imag),
                    imag - (own_real * pivot_imag + own_imag * pivot_real),
                )

            row_real = jnp.where(hit, jnp.where(here, 1.0, 0.0), row_real)
            row_imag = jnp.where(hit, 0.0, row_imag)
            row_real, row_imag = reduce(row_real, row_imag)
            for j in columns:
                columns[j] = reduce(*columns[j])
        rows = jnp.concatenate([row_real, row_imag], axis=1)
        extra = jnp.where(lane == base + sublane, 1.0, 0.0)
        high, low = split(jnp.concatenate([row_real + extra, row_imag], axis=1))
        turned_high = jnp.concatenate([-high[:, TILE:], high[:, :TILE]], axis=1)
        turned_low = jnp.concatenate([-low[:, TILE:], low[:, :TILE]], axis=1)
        right = [high, turned_high, high, turned_high, low, turned_low]
        right += [jnp.zeros_like(low)] * (TILE // PANEL - len(right))
        update = dot(left, jnp.concatenate(right, axis=0))
        tile[:, :TILE] = real - update[:, :TILE]
        tile[:, TILE:] = imag - update[:, TILE:]
        tile[pl.ds(base, PANEL), :] = rows
        return 0

    lax.fori_loop(0, TILE // PANEL, panel, 0)


def step_kernel(
    pairs, shots, where_ref, mine_any, other_any, steering_any, high_any, low_any, out_ref,
    mine_ref, other_ref, steering_ref, high_ref, low_ref, matrix, tile, inv_high, inv_low, copied
):
    order = matrix.shape[0]
    blocks = order // TILE
    owned = steering_ref.shape[2]
    per = steering_any.shape[3] // owned
    column = pl.multiple_of((where_ref[0] % per) * owned, owned)
    own_steering = steering_any.at[where_ref[0] // per, :, :, pl.ds(column, owned)]
    sources = [mine_any, other_any, own_steering, high_any, low_any]
    targets = [mine_ref, other_ref, steering_ref, high_ref, low_ref]
    copies = [pltpu.make_async_copy(a, b, copied.at[n]) for n, (a, b) in enumerate(zip(sources, targets))]
    for copy in copies:
        copy.start()
    for copy in copies[:2]:
        copy.wait()

    def rows(i):
        return slice(i * TILE, (i + 1) * TILE)

    def cols(i, part):
        return slice(part * order + i * TILE, part * order + (i + 1) * TILE)

    def put(group, ref):
        for index, (a, b) in enumerate(pairs[group]):
            real, imag = ref[2 * index], ref[2 * index + 1]
            if a == b:
                matrix[rows(a), cols(a, 0)] = 0.5 * (real + real.T)
                matrix[rows(a), cols(a, 1)] = 0.5 * (imag - imag.T)
            else:
                matrix[rows(a), cols(b, 0)] = real
                matrix[rows(a), cols(b, 1)] = imag
                matrix[rows(b), cols(a, 0)] = real.T
                matrix[rows(b), cols(a, 1)] = -imag.T

    @pl.when(where_ref[1] == 0)
    def _():
        put(0, mine_ref)
        put(1, other_ref)

    @pl.when(where_ref[1] != 0)
    def _():
        put(1, mine_ref)
        put(0, other_ref)

    diagonal = lax.broadcasted_iota(jnp.int32, (TILE, TILE), 0) == lax.broadcasted_iota(jnp.int32, (TILE, TILE), 1)
    trace = jnp.zeros((1, 1), F32)
    for i in range(blocks):
        kept = jnp.where(diagonal, matrix[rows(i), cols(i, 0)], 0.0)
        trace = trace + jnp.sum(jnp.sum(kept, axis=0, keepdims=True), axis=1, keepdims=True)
    matrix[...] = matrix[...] * (1.0 / trace)
    for i in range(blocks):
        matrix[rows(i), cols(i, 0)] += jnp.where(diagonal, 1.0 / order, 0.0)

    unit = jnp.where(diagonal, 1.0, 0.0)
    nothing = jnp.zeros((TILE, TILE), F32)
    for k in range(blocks):
        tile[:, :TILE] = matrix[rows(k), cols(k, 0)]
        tile[:, TILE:] = matrix[rows(k), cols(k, 1)]
        invert_tile(tile)
        column = jnp.concatenate([matrix[:, cols(k, 0)], matrix[:, cols(k, 1)]], axis=1)
        matrix[rows(k), cols(k, 0)] = unit
        matrix[rows(k), cols(k, 1)] = nothing
        row_real, row_imag = matrix[rows(k), :order], matrix[rows(k), order:]
        panel = jnp.concatenate([row_real, row_imag], axis=1)
        turned = jnp.concatenate([-row_imag, row_real], axis=1)
        row = dot3(tile[...], jnp.concatenate([panel, turned], axis=0))
        row_turned = jnp.concatenate([-row[:, order:], row[:, :order]], axis=1)
        tall = jnp.concatenate([row, row_turned], axis=0)
        for i in range(blocks):
            if i == k:
                matrix[rows(k), :] = row
            else:
                matrix[rows(i), cols(k, 0)] = nothing
                matrix[rows(i), cols(k, 1)] = nothing
                matrix[rows(i), :] -= dot3(column[rows(i)], tall)

    weights = []
    lane = lax.broadcasted_iota(jnp.int32, (TILE, 2 * order), 1)
    sublane = lax.broadcasted_iota(jnp.int32, (TILE, 2 * order), 0)
    for i in range(blocks):
        on_diagonal = lane == sublane + i * TILE
        found = matrix[rows(i), :]
        weights.append(jnp.sum(jnp.where(on_diagonal, found, 0.0), axis=1, keepdims=True))
        inv_high[rows(i), :], inv_low[rows(i), :] = split(jnp.where(on_diagonal, 0.0, found))
    for copy in copies[2:]:
        copy.wait()

    def turn(pair):
        return jnp.concatenate([pair, jnp.concatenate([-pair[:, owned:], pair[:, :owned]], axis=1)], axis=0)

    def over_channels(pair):
        total = jnp.sum(pair, axis=0, keepdims=True)
        return total[:, :owned] + total[:, owned:]

    vectors = jnp.concatenate(
        [jnp.concatenate([steering_ref[b, :TILE, :], steering_ref[b, TILE:, :]], axis=1) for b in range(blocks)], axis=0
    )
    wide = vectors.astype(F32)
    right = turn(vectors)
    solved = dot(inv_high[...], right) + dot(inv_low[...], right) + jnp.concatenate(weights, axis=0) * wide
    norms = over_channels(solved * wide)
    right = turn(solved.astype(BF16))
    turned = dot(high_ref[...], right) + dot(low_ref[...], right)
    out_ref[...] = over_channels(turned * solved) / (shots * norms * norms)


def next_powers(where, mine, other, steering, sample, owned, pairs, shots):
    blocks = steering.shape[1]
    order = blocks * TILE
    half = pltpu.VMEM((order, 2 * order), BF16)
    operands = (mine, other, steering, *sample)
    grid_spec = pltpu.PrefetchScalarGridSpec(
        num_scalar_prefetch=1,
        grid=(1,),
        in_specs=[pl.BlockSpec(memory_space=pl.ANY)] * len(operands),
        out_specs=pl.BlockSpec((1, owned), lambda s, m: (0, 0)),
        scratch_shapes=[
            pltpu.VMEM(mine.shape, F32),
            pltpu.VMEM(other.shape, F32),
            pltpu.VMEM((blocks, PAIR, owned), BF16),
            half,
            half,
            pltpu.VMEM((order, 2 * order), F32),
            pltpu.VMEM((TILE, PAIR), F32),
            half,
            half,
            pltpu.SemaphoreType.DMA((len(operands),)),
        ],
    )
    return pl.pallas_call(
        functools.partial(step_kernel, pairs, shots),
        grid_spec=grid_spec,
        out_shape=jax.ShapeDtypeStruct((1, owned), F32),
        name="step",
        cost_estimate=cost(28),
        compiler_params=pltpu.CompilerParams(vmem_limit_bytes=56 * 1024 * 1024),
    )(where, *operands)


def shards(cube, select, phases, jitter):
    snap_count, ang_count = lax.axis_size("snap"), lax.axis_size("ang")
    snap_index, ang_index = lax.axis_index("snap"), lax.axis_index("ang")
    channels = cube.shape[1]
    shots = select.shape[0] * snap_count
    owned = K // (ang_count * snap_count)
    groups = block_groups(channels // TILE)
    pairs = [group_pairs(group) for group in groups]
    slots = [slot for slot, (a, partners) in enumerate(groups[0]) for b in partners]
    core = snap_index % 2
    me = (ang_index * snap_count + snap_index).astype(jnp.int32)
    where = jnp.stack([me, core.astype(jnp.int32)])
    flat = [
        jnp.array([a for a, partners in group] + [b for a, b in group_pairs(group)], jnp.int32) for group in groups
    ]
    table = jnp.concatenate([me[None], jnp.where(core == 0, flat[0], flat[1])])

    width = max(owned, WIDTH)
    tables = angle_tables(phases, jitter, width // GV)
    every = [(a, b) for a in range(channels // TILE) for b in range(a + 1)]
    keep, give, rows = sample_terms(where, cube, select - snap_index * cube.shape[2], every)
    piece = (keep + swap(give, "snap", 1)).reshape(-1, TILE)
    for bit in range(1, snap_count.bit_length() - 1):
        piece = halve(piece, "snap", bit)
    steering, energy = fill_steering(where, tables, channels // TILE, owned, width, 0, shots=rows)
    powers = scatter_energy(energy.reshape(snap_count, owned)) / float(shots * channels * channels)
    for mask in range(1, ang_count):
        (steering,) = fill_steering(
            where, tables, channels // TILE, owned, width, mask, before=steering
        )
    gathered = gather_relative(powers)

    def iteration(gathered):
        mine = covariance_half(table, steering, gathered, slots)
        other = swap(mine, "snap", 1)
        return next_powers(where, mine, other, steering, sample, owned, pairs, float(shots))

    gathered, piece = lax.optimization_barrier((gathered, piece))
    others = []
    for m in range(2, snap_count, 2):
        others.append(swap(piece, "snap", m))
    both = jnp.concatenate([piece] + others, axis=0)
    sample = spread(where, [both, swap(both, "snap", 1)], every, channels)
    powers = iteration(gathered)
    return lax.fori_loop(1, ITERS, lambda _, powers: iteration(gather_relative(powers)), powers)[0]


def solution(mesh):
    return jax.shard_map(
        shards,
        mesh=mesh,
        in_specs=(P(None, None, "snap"), P("snap"), P(), P()),
        out_specs=P(("ang", "snap")),
        check_vma=False,
    )
```
